32 devices in a mesh: dop: 2 (over y), rng: 16 (over z, x, core).
Axes of the slice: x: 2, y: 2, z: 4, core: 2. Of those that a mesh axis runs over, the one named last changes fastest.
Arguments:
- radar_cube: bfloat16 [2, 128, 1024, 512], P(None, 'dop', 'rng'), may hold values from -40 to 40
- train_gates: int32 [2, 768], P('dop', 'rng'), may hold values from 0 to 63, as said below
- look_angles: int32 [2, 8], P('dop'), may hold values from 0 to 255
Outputs:
- filtered: float32 [2, 2, 8, 1024], P(None, 'dop', None, 'rng')
The draws below stay inside these ranges and needn't reach their ends.
Inputs may be any that keep to these rules, and one draw needn't show every extreme that they name: `train_gates`: entries k * 48 to (k + 1) * 48 - 1 of a bin's row list in increasing order the gates of the k-th block of 64 consecutive range gates, counted from that block's first gate, that lie outside one run of 16 consecutive gates of the block.
All inputs are finite; a program needn't handle non-finite values.
Results may differ from the reference program's by a relative error of at most 0.014.
The reference program's roundings to bfloat16 on the way count: a program that leaves them out, or rounds other values in their place, can miss the bound.
Values may be sent and summed in bfloat16 or wider, within the bound.
No kernel may reach another device: no remote copies, remote signals or barrier semaphores. Data moves between devices by JAX's collectives and lax.ppermute only.
A program may use at most 64 MiB of HBM per device.

```python
import math
import jax
import jax.numpy as jnp
from jax import lax

C = 512
P_SIZE = 128
NANG = 256
BEAMS = 8
G_DEV = 64
GUARD = 16
TR_DEV = 48
NB = 2
GATES = 1024
TRAIN = 768


def draw_radar_cube(key, part):
    subkeys = jax.random.split(key, 5)
    source_count = 16
    gains = jnp.exp(jax.random.uniform(subkeys[0], (C,), minval=math.log(0.5), maxval=math.log(2.0)))
    directions = jax.random.uniform(subkeys[1], (source_count,), minval=-1.0, maxval=1.0)
    powers = jnp.exp(jax.random.uniform(subkeys[2], (source_count,), minval=math.log(0.5), maxval=math.log(4.0))) * (6.0 / source_count)
    phase = math.pi * jnp.arange(C, dtype=jnp.float32)[:, None] * directions[None, :]
    steer_real = jnp.cos(phase)
    steer_imag = jnp.sin(phase)
    amplitude = jax.random.normal(subkeys[3], (2, P_SIZE, GATES, source_count), dtype=jnp.float32) * jnp.sqrt(powers / 2.0)
    clutter_real = jnp.einsum('pgk,ck->pgc', amplitude[0], steer_real) - jnp.einsum('pgk,ck->pgc', amplitude[1], steer_imag)
    clutter_imag = jnp.einsum('pgk,ck->pgc', amplitude[0], steer_imag) + jnp.einsum('pgk,ck->pgc', amplitude[1], steer_real)
    clutter = jnp.stack([clutter_real, clutter_imag])
    noise = jax.random.normal(subkeys[4], (2, P_SIZE, GATES, C), dtype=jnp.float32)
    samples = (noise + clutter) * gains[None, None, None, :]
    return jnp.clip(samples, -40.0, 40.0).astype(jnp.bfloat16)


def draw_train_gates(key, part):
    block_count = TRAIN // TR_DEV
    starts = jax.random.randint(key, (NB, block_count, 1), 0, G_DEV - GUARD + 1)
    offsets = jnp.arange(TR_DEV, dtype=jnp.int32)[None, None, :]
    gate_index = offsets + GUARD * (offsets >= starts).astype(jnp.int32)
    return gate_index.reshape(NB, TRAIN).astype(jnp.int32)


def set_ends(result, own_key, smallest, largest):
    shape = result.shape
    spot = [jax.random.randint(jax.random.fold_in(own_key, axis), (), 0, shape[axis]) for axis in range(len(shape))]
    result = result.at[tuple(spot)].set(smallest)
    longest = shape.index(max(shape))
    spot[longest] = (spot[longest] + 1) % shape[longest]
    return result.at[tuple(spot)].set(largest)


def setup_inputs(seed: int = 0) -> dict:
    streams_of = jax.random.split(jax.random.key(seed), 4)
    return {
        "radar_cube": draw_radar_cube(jax.random.fold_in(streams_of[3], 71), 0),
        "train_gates": draw_train_gates(jax.random.fold_in(streams_of[3], 71), 0),
        "look_angles": set_ends(jax.random.randint(streams_of[2], (NB, BEAMS), 0, NANG), jax.random.fold_in(streams_of[2], 1), 0, NANG - 1).astype(jnp.int32),
    }


load_eps = 1e-05

def doppler_table(bin_count, pulses):
    bin_freq = jnp.arange(bin_count, dtype=jnp.int32) * (pulses // bin_count)
    pulse_index = jnp.arange(pulses, dtype=jnp.int32)
    phase = (bin_freq[:, None] * pulse_index[None, :] % pulses).astype(jnp.float32) * (2.0 * math.pi / pulses)
    cosine = jnp.cos(phase).astype(jnp.bfloat16)
    sine = jnp.sin(phase).astype(jnp.bfloat16)
    upper = jnp.concatenate([cosine, sine], 1)
    lower = jnp.concatenate([-sine, cosine], 1)
    return jnp.concatenate([upper, lower], 0)

def gram_terms(train_rows):
    real_part = train_rows[0]
    imag_part = train_rows[1]
    contract = (((0,), (0,)), ((), ()))
    stacked = jnp.concatenate([real_part, imag_part], 0)
    power_sum = lax.dot_general(stacked.astype(jnp.float32), stacked.astype(jnp.float32), contract, preferred_element_type=jnp.float32)
    left_rows = jnp.concatenate([real_part, -imag_part], 0)
    right_rows = jnp.concatenate([imag_part, real_part], 0)
    cross_sum = lax.dot_general(left_rows.astype(jnp.float32), right_rows.astype(jnp.float32), contract, preferred_element_type=jnp.float32)
    return (power_sum, cross_sum)

def solve_weights(power_sum, cross_sum, look_row, train_count, angle_count):
    channels = power_sum.shape[0]
    top_half = jnp.concatenate([power_sum, cross_sum], 1)
    bottom_half = jnp.concatenate([cross_sum.T, power_sum], 1)
    covariance = jnp.concatenate([top_half, bottom_half], 0) / train_count
    loading = load_eps * jnp.trace(covariance) / (2 * channels)
    covariance = covariance + loading * jnp.eye(2 * channels, dtype=jnp.float32)
    factor = jnp.linalg.cholesky(covariance)
    channel_index = jnp.arange(channels, dtype=jnp.int32)
    slope = 2 * look_row.astype(jnp.int32) + 1 - angle_count
    modulus = channel_index[:, None] * slope[None, :] % (2 * angle_count)
    phase = modulus.astype(jnp.float32) * (math.pi / angle_count)
    steering = jnp.concatenate([jnp.cos(phase), jnp.sin(phase)], 0)
    whitened = jax.scipy.linalg.solve_triangular(factor, steering, lower=True)
    lengths = jnp.sqrt(lax.optimization_barrier(jnp.sum(whitened * whitened, axis=0)))
    weights = jax.scipy.linalg.solve_triangular(factor, whitened / lengths[None, :], trans=1, lower=True)
    return weights.astype(jnp.bfloat16)

def filter_gates(spectrum, weights):
    direct = jnp.concatenate([spectrum[0], spectrum[1]], 1)
    rotated = jnp.concatenate([-spectrum[1], spectrum[0]], 1)
    contract = (((0,), (1,)), ((), ()))
    real_out = lax.dot_general(weights.astype(jnp.float32), direct.astype(jnp.float32), contract, preferred_element_type=jnp.float32)
    imag_out = lax.dot_general(weights.astype(jnp.float32), rotated.astype(jnp.float32), contract, preferred_element_type=jnp.float32)
    return jnp.stack([real_out, imag_out])

def reference(radar_cube, train_gates, look_angles):
    dft_table = doppler_table(NB, P_SIZE)
    flattened = radar_cube.reshape(2 * P_SIZE, GATES * C)
    spectral = (jnp.dot(dft_table.astype(jnp.float32), flattened.astype(jnp.float32), preferred_element_type=jnp.float32) * (1.0 / math.sqrt(P_SIZE))).astype(jnp.bfloat16)
    spectral = spectral.reshape(2, NB, GATES, C)
    block_offset = jnp.arange(TRAIN, dtype=jnp.int32) // TR_DEV * G_DEV

    def per_bin(bin_index):
        spectrum = spectral[:, bin_index]
        gate_list = train_gates[bin_index].astype(jnp.int32) + block_offset
        train_rows = jnp.take(spectrum, gate_list, axis=1)
        power_sum, cross_sum = gram_terms(train_rows)
        weights = solve_weights(power_sum, cross_sum, look_angles[bin_index], TRAIN, NANG)
        return filter_gates(spectrum, weights)
    outcome = lax.map(per_bin, jnp.arange(NB, dtype=jnp.int32))
    return jnp.transpose(outcome, (1, 0, 2, 3))
```

```python
import math

import jax
import jax.numpy as jnp
import numpy as np
from jax import lax
from jax.experimental import pallas as pl
from jax.experimental.pallas import tpu as pltpu
from jax.sharding import PartitionSpec as P

NANG = 256
LOAD_EPS = 1e-05
HALF = 64
LANES = 128
SUB = 8
HIGH = lax.Precision.HIGHEST


def doppler_table(bin_count, pulses):
    phase = (np.arange(bin_count)[:, None] * (pulses // bin_count) * np.arange(pulses)[None, :] % pulses) * (
        2.0 * math.pi / pulses
    )
    cosine = jnp.asarray(np.cos(phase), jnp.float32).astype(jnp.bfloat16).astype(jnp.float32)
    sine = jnp.asarray(np.sin(phase), jnp.float32).astype(jnp.bfloat16).astype(jnp.float32)
    upper = jnp.stack([cosine, sine], 1)
    lower = jnp.stack([-sine, cosine], 1)
    return jnp.stack([upper, lower], 0)


def partial_kernel(classes, outs, coef_ref, cube_ref, out_ref):
    local = cube_ref.shape[1]
    folded = []
    for part in range(2):
        for cls in range(classes):
            total = cube_ref[part, cls].astype(jnp.float32)
            for pulse in range(cls + classes, local, classes):
                total = total + cube_ref[part, pulse].astype(jnp.float32)
            folded.append(total)
    for row in range(outs):
        acc = folded[0] * coef_ref[row, 0]
        for col in range(1, 2 * classes):
            acc = acc + folded[col] * coef_ref[row, col]
        out_ref[row] = acc


def partial_spectra(cube, coef, classes):
    _, local, gates, channels = cube.shape
    rows = coef.shape[0]
    step = 16
    width = min(channels, 256)
    return pl.pallas_call(
        lambda *refs: partial_kernel(classes, rows, *refs),
        grid=(gates // step, channels // width),
        in_specs=[
            pl.BlockSpec(memory_space=pltpu.SMEM),
            pl.BlockSpec((2, local, step, width), lambda i, j: (0, 0, i, j)),
        ],
        out_specs=pl.BlockSpec((rows, step, width), lambda i, j: (0, i, j)),
        out_shape=jax.ShapeDtypeStruct((rows, gates, channels), jnp.float32),
        name="partial_spectra",
    )(coef, cube)


def finish_kernel(scale, *refs):
    gates_ref, *parts, spec_ref, pack_ref = refs
    train = gates_ref.shape[1]
    gates = spec_ref.shape[1]
    shift = gates - train
    index = lax.broadcasted_iota(jnp.int32, (1, train), 1)
    same = jnp.where(gates_ref[...] == index, 1.0, 0.0)
    start = jnp.sum(same, axis=1, keepdims=True)
    row = lax.broadcasted_iota(jnp.int32, (train, LANES), 0).astype(jnp.float32)
    early = row < start
    lane = lax.broadcasted_iota(jnp.int32, (train, LANES), 1)
    low = lane < HALF
    for tile in range(spec_ref.shape[2] // LANES):
        cols = slice(tile * LANES, (tile + 1) * LANES)
        picked = []
        for part in range(2):
            total = parts[0][part, :, cols]
            for other in parts[1:]:
                total = total + other[part, :, cols]
            value = (total * scale).astype(jnp.bfloat16)
            spec_ref[part, :, cols] = value
            value = value.astype(jnp.float32)
            picked.append(jnp.where(early, value[:train], value[shift:]))
        real, imag = picked
        first = jnp.where(low, real, pltpu.roll(imag, HALF, 1))
        second = jnp.where(low, pltpu.roll(real, HALF, 1), imag)
        base = 2 * tile * LANES
        pack_ref[:, base : base + LANES] = first.astype(jnp.bfloat16)
        pack_ref[:, base + LANES : base + 2 * LANES] = second.astype(jnp.bfloat16)


def finish_spectra(gate_row, parts, scale):
    _, gates, channels = parts[0].shape
    train = gate_row.shape[1]
    return pl.pallas_call(
        lambda *refs: finish_kernel(scale, *refs),
        out_shape=(
            jax.ShapeDtypeStruct((2, gates, channels), jnp.bfloat16),
            jax.ShapeDtypeStruct((train, 2 * channels), jnp.bfloat16),
        ),
        name="finish_spectra",
    )(gate_row, *parts)


def spread(value, row):
    return jnp.broadcast_to(value[row : row + 1, :], (SUB, LANES))


def lane_spread(value, lane):
    return jnp.broadcast_to(value[:, lane : lane + 1], (SUB, LANES))


def tree_sum(terms):
    terms = list(terms)
    while len(terms) > 1:
        nxt = [terms[i] + terms[i + 1] for i in range(0, len(terms) - 1, 2)]
        if len(terms) % 2:
            nxt.append(terms[-1])
        terms = nxt
    return terms[0]


def invert_rows(real_cols, imag_cols, rows, turned, sub):
    scale = None
    for j in range(SUB):
        recip = 1.0 / spread(real_cols[j], j)
        own = sub == j
        scale = recip if scale is None else jnp.where(own, recip, scale)
        sr = jnp.where(own, 0.0, real_cols[j] * recip)
        si = jnp.where(own, 0.0, imag_cols[j] * recip)
        for l in range(j + 1, SUB):
            ur = spread(real_cols[l], j)
            ui = spread(imag_cols[l], j)
            real_cols[l] = real_cols[l] - (sr * ur - si * ui)
            imag_cols[l] = imag_cols[l] - (sr * ui + si * ur)
        one = spread(rows, j)
        two = spread(turned, j)
        rows = rows - (sr * one + si * two)
        turned = turned - (sr * two - si * one)
    return rows * scale, turned * scale


def invert_block(tiles, lane, sub, sign):
    count = len(tiles)
    for t in range(count):
        k = SUB * t
        in_re = (lane >= k) & (lane < k + SUB)
        in_im = (lane >= HALF + k) & (lane < HALF + k + SUB)
        inside = in_re | in_im
        real_cols = [lane_spread(tiles[t], k + l) for l in range(SUB)]
        imag_cols = [lane_spread(tiles[t], HALF + k + l) for l in range(SUB)]
        unit = jnp.where(in_re & (lane - k == sub), 1.0, 0.0)
        rows = jnp.where(inside, unit, tiles[t])
        turned = pltpu.roll(rows, HALF, 1) * sign
        rows, turned = invert_rows(real_cols, imag_cols, rows, turned, sub)
        ones = [spread(rows, l) for l in range(SUB)]
        twos = [spread(turned, l) for l in range(SUB)]
        fresh = list(tiles)
        fresh[t] = rows
        for i in list(range(t + 1, count)) + list(range(t)):
            terms = []
            for l in range(SUB):
                cr = lane_spread(tiles[i], k + l)
                ci = lane_spread(tiles[i], HALF + k + l)
                terms.append(cr * ones[l] + ci * twos[l])
            fresh[i] = jnp.where(inside, 0.0, tiles[i]) - tree_sum(terms)
        tiles = fresh
    return tiles


def turn(value, sign):
    tiles = value.shape[1] // LANES
    out = [
        pltpu.roll(value[:, t * LANES : (t + 1) * LANES], HALF, 1) * sign[: value.shape[0]]
        for t in range(tiles)
    ]
    return out[0] if tiles == 1 else jnp.concatenate(out, 1)


def exact_dot(a, b):
    return jnp.dot(a, b, precision=HIGH, preferred_element_type=jnp.float32)


def solve_kernel(train_count, beams, gram_ref, steer_ref, spec_ref, out_ref, mat, xs):
    blocks = gram_ref.shape[0] // LANES
    lane = lax.broadcasted_iota(jnp.int32, (SUB, LANES), 1)
    sub = lax.broadcasted_iota(jnp.int32, (SUB, LANES), 0)
    sign = jnp.where(lane < HALF, -1.0, 1.0)
    blane = lax.broadcasted_iota(jnp.int32, (HALF, LANES), 1)
    brow = lax.broadcasted_iota(jnp.int32, (HALF, LANES), 0)
    bsign = jnp.where(blane < HALF, -1.0, 1.0)
    inv = 1.0 / train_count
    diag = blane == brow
    trace = jnp.zeros((HALF, LANES), jnp.float32)
    for i in range(blocks):
        for j in range(blocks):
            top = gram_ref[i * LANES : i * LANES + HALF, j * LANES : (j + 1) * LANES]
            low = gram_ref[i * LANES + HALF : (i + 1) * LANES, j * LANES : (j + 1) * LANES]
            value = (pltpu.roll(low, HALF, 1) - top * bsign) * inv
            mat[i * HALF : (i + 1) * HALF, j * LANES : (j + 1) * LANES] = value
            if i == j:
                trace = trace + jnp.where(diag, value, 0.0)
        mat[i * HALF : (i + 1) * HALF, blocks * LANES :] = steer_ref[i * HALF : (i + 1) * HALF, :]
    load = LOAD_EPS * jnp.sum(trace, keepdims=True) / (blocks * HALF)
    for i in range(blocks):
        at = (slice(i * HALF, (i + 1) * HALF), slice(i * LANES, (i + 1) * LANES))
        mat[at] = mat[at] + jnp.where(diag, load, 0.0)

    norm = jnp.zeros((HALF, LANES), jnp.float32)
    for k in range(blocks):
        rows = slice(k * HALF, (k + 1) * HALF)
        tiles = [
            mat[k * HALF + SUB * t : k * HALF + SUB * (t + 1), k * LANES : (k + 1) * LANES]
            for t in range(HALF // SUB)
        ]
        inverse = jnp.concatenate(invert_block(tiles, lane, sub, sign), 0)
        right = mat[rows, (k + 1) * LANES :]
        upper = exact_dot(inverse, jnp.concatenate([right, turn(right, bsign)], 0))
        norm = norm + right[:, -LANES:] * upper[:, -LANES:]
        mat[rows, (k + 1) * LANES :] = upper
        if k + 1 < blocks:
            below = slice((k + 1) * HALF, blocks * HALF)
            both = jnp.concatenate([upper, turn(upper, bsign)], 0)
            mat[below, (k + 1) * LANES :] = mat[below, (k + 1) * LANES :] - exact_dot(
                mat[below, k * LANES : (k + 1) * LANES], both
            )
    total = jnp.sum(norm, axis=0, keepdims=True)
    total = total + pltpu.roll(jnp.broadcast_to(total, (SUB, LANES)), HALF, 1)[:1]
    low8 = (blane[:1] % HALF) < beams
    factor = jnp.where(low8, lax.rsqrt(jnp.where(low8, total, 1.0)), 0.0)
    for k in reversed(range(blocks)):
        rows = slice(k * HALF, (k + 1) * HALF)
        value = mat[rows, blocks * LANES :]
        if k + 1 < blocks:
            value = value - exact_dot(
                mat[rows, (k + 1) * LANES : blocks * LANES], xs[(k + 1) * LANES : blocks * LANES, :]
            )
        xs[k * LANES : k * LANES + HALF, :] = value
        xs[k * LANES + HALF : (k + 1) * LANES, :] = turn(value, bsign)
    weights = jnp.concatenate(
        [(xs[k * LANES : k * LANES + HALF, :] * factor).astype(jnp.bfloat16) for k in range(blocks)], 0
    )
    contract = (((0,), (1,)), ((), ()))
    real = lax.dot_general(weights, spec_ref[0], contract, preferred_element_type=jnp.float32)
    imag = lax.dot_general(weights, spec_ref[1], contract, preferred_element_type=jnp.float32)
    out_ref[0] = real[:beams] + imag[HALF : HALF + beams]
    out_ref[1] = real[HALF : HALF + beams] - imag[:beams]


def solve_and_filter(gram, steer, spectrum, train_count, beams):
    channels = gram.shape[0] // 2
    gates = spectrum.shape[1]
    return pl.pallas_call(
        lambda *refs: solve_kernel(train_count, beams, *refs),
        out_shape=jax.ShapeDtypeStruct((2, beams, gates), jnp.float32),
        scratch_shapes=[
            pltpu.VMEM((channels, 2 * channels + LANES), jnp.float32),
            pltpu.VMEM((2 * channels, LANES), jnp.float32),
        ],
        name="solve_and_filter",
    )(gram, steer, spectrum)


def packed_steering(look_row, channels, angle_count):
    beams = look_row.shape[0]
    slope = 2 * look_row + 1 - angle_count
    half = jnp.pad(slope, (0, HALF - beams))
    lane = jnp.arange(LANES, dtype=jnp.int32)
    channel = jnp.arange(channels, dtype=jnp.int32)
    index = channel[:, None] * jnp.concatenate([half, half])[None, :]
    index = (index - jnp.where(lane >= HALF, angle_count // 2, 0)[None, :]) % (2 * angle_count)
    value = jnp.cos(index.astype(jnp.float32) * (math.pi / angle_count))
    return jnp.where((lane % HALF < beams)[None, :], value, 0.0)


def on_device(radar_cube, train_gates, look_angles):
    dop = lax.axis_size("dop")
    rng = lax.axis_size("rng")
    me = lax.axis_index("dop")
    local = radar_cube.shape[1]
    pulses = local * dop
    channels = radar_cube.shape[3]
    bins = dop * train_gates.shape[0]
    beams = look_angles.shape[1]
    classes = bins if local % bins == 0 else local
    table = doppler_table(bins, pulses)
    table = lax.dynamic_slice_in_dim(table, me * local, classes, axis=3)
    table = jnp.roll(table, -me, axis=1)
    coef = jnp.transpose(table, (1, 0, 2, 3)).reshape(2 * bins, 2 * classes)
    parts = partial_spectra(radar_cube, coef, classes)
    parts = parts.reshape(bins, 2, *parts.shape[1:])
    mine = [parts[0]]
    for hop in range(1, dop):
        pairs = [(d, (d + hop) % dop) for d in range(dop)]
        mine.append(lax.ppermute(parts[hop], "dop", pairs))
    spectrum, packed = finish_spectra(train_gates, mine, 1.0 / math.sqrt(pulses))
    gathered = lax.all_gather(packed, "rng", axis=0, tiled=True)
    gram = lax.dot_general(
        gathered, gathered, (((0,), (0,)), ((), ())), preferred_element_type=jnp.float32
    )
    steer = packed_steering(look_angles[0], channels, NANG)
    out = solve_and_filter(gram, steer, spectrum, train_gates.shape[1] * rng, beams)
    return out[:, None]


def solution(mesh):
    placed = (P(None, "dop", "rng", None), P("dop", "rng"), P("dop", None))
    return jax.shard_map(
        on_device,
        mesh=mesh,
        in_specs=placed,
        out_specs=P(None, "dop", None, "rng"),
        check_vma=False,
    )
```

```python
import math

import jax
import jax.numpy as jnp
import numpy as np
from jax import lax
from jax.experimental import pallas as pl
from jax.experimental.pallas import tpu as pltpu
from jax.sharding import PartitionSpec as P

NANG = 256
LOAD_EPS = 1e-05
HALF = 64
LANES = 128
SUB = 8
HIGH = lax.Precision.HIGHEST


def doppler_table(bin_count, pulses):
    phase = (np.arange(bin_count)[:, None] * (pulses // bin_count) * np.arange(pulses)[None, :] % pulses) * (
        2.0 * math.pi / pulses
    )
    cosine = np.cos(phase).astype(np.float32).astype(jnp.bfloat16).astype(np.float32)
    sine = np.sin(phase).astype(np.float32).astype(jnp.bfloat16).astype(np.float32)
    upper = np.stack([cosine, sine], 1)
    lower = np.stack([-sine, cosine], 1)
    return np.stack([upper, lower], 0)


def pick(values, index):
    if all(v == values[0] for v in values):
        return float(values[0])
    out = jnp.float32(values[0])
    for i, v in enumerate(values[1:], 1):
        out = jnp.where(index == i, jnp.float32(v), out)
    return out


def partial_kernel(classes, dop, table, *refs):
    cube_ref, *out_refs = refs
    me = lax.axis_index("dop")
    local, _, width = cube_ref.shape[1:]
    for base in range(0, width, LANES):
        cols = slice(base, base + LANES)
        folded = []
        for part in range(2):
            for cls in range(classes):
                total = cube_ref[part, cls, :, cols].astype(jnp.float32)
                for pulse in range(cls + classes, local, classes):
                    total = total + cube_ref[part, pulse, :, cols].astype(jnp.float32)
                folded.append(total)
        for slot, out_ref in enumerate(out_refs):
            for row in range(2):
                acc = None
                for part in range(2):
                    for cls in range(classes):
                        options = [
                            table[row, (d + slot) % dop, part, d * local + cls] for d in range(dop)
                        ]
                        term = folded[part * classes + cls] * pick(options, me)
                        acc = term if acc is None else acc + term
                out_ref[row, :, cols] = acc


def partial_spectra(cube, table, classes, dop):
    _, local, gates, channels = cube.shape
    step = 16
    return pl.pallas_call(
        lambda *refs: partial_kernel(classes, dop, table, *refs),
        grid=(gates // step,),
        in_specs=[pl.BlockSpec((2, local, step, channels), lambda i: (0, 0, i, 0))],
        out_specs=[pl.BlockSpec((2, step, channels), lambda i: (0, i, 0))] * dop,
        out_shape=[jax.ShapeDtypeStruct((2, gates, channels), jnp.float32)] * dop,
        name="partial_spectra",
    )(cube)


def finish_kernel(scale, *refs):
    gates_ref, *parts, spec_ref, pack_ref = refs
    train = gates_ref.shape[1]
    gates = spec_ref.shape[1]
    shift = gates - train
    index = lax.broadcasted_iota(jnp.int32, (1, train), 1)
    same = jnp.where(gates_ref[...] == index, 1.0, 0.0)
    start = jnp.sum(same, axis=1, keepdims=True)
    row = lax.broadcasted_iota(jnp.int32, (train, LANES), 0).astype(jnp.float32)
    early = row < start
    lane = lax.broadcasted_iota(jnp.int32, (train, LANES), 1)
    low = lane < HALF
    for tile in range(spec_ref.shape[2] // LANES):
        cols = slice(tile * LANES, (tile + 1) * LANES)
        picked = []
        for part in range(2):
            total = parts[0][part, :, cols]
            for other in parts[1:]:
                total = total + other[part, :, cols]
            value = (total * scale).astype(jnp.bfloat16)
            spec_ref[part, :, cols] = value
            value = value.astype(jnp.float32)
            picked.append(jnp.where(early, value[:train], value[shift:]))
        real, imag = picked
        first = jnp.where(low, real, pltpu.roll(imag, HALF, 1))
        second = jnp.where(low, pltpu.roll(real, HALF, 1), imag)
        base = 2 * tile * LANES
        pack_ref[:, base : base + LANES] = first.astype(jnp.bfloat16)
        pack_ref[:, base + LANES : base + 2 * LANES] = second.astype(jnp.bfloat16)


def finish_spectra(gate_row, parts, scale):
    _, gates, channels = parts[0].shape
    train = gate_row.shape[1]
    return pl.pallas_call(
        lambda *refs: finish_kernel(scale, *refs),
        out_shape=(
            jax.ShapeDtypeStruct((2, gates, channels), jnp.bfloat16),
            jax.ShapeDtypeStruct((train, 2 * channels), jnp.bfloat16),
        ),
        name="finish_spectra",
    )(gate_row, *parts)


def spread(value, row):
    return jnp.broadcast_to(value[row : row + 1, :], (SUB, LANES))


def lane_spread(value, lane):
    return jnp.broadcast_to(value[:, lane : lane + 1], (SUB, LANES))


def tree_sum(terms):
    terms = list(terms)
    while len(terms) > 1:
        nxt = [terms[i] + terms[i + 1] for i in range(0, len(terms) - 1, 2)]
        if len(terms) % 2:
            nxt.append(terms[-1])
        terms = nxt
    return terms[0]


def invert_rows(real_cols, imag_cols, rows, turned, sub):
    scale = None
    for j in range(SUB):
        recip = 1.0 / spread(real_cols[j], j)
        own = sub == j
        scale = recip if scale is None else jnp.where(own, recip, scale)
        sr = jnp.where(own, 0.0, real_cols[j] * recip)
        si = jnp.where(own, 0.0, imag_cols[j] * recip)
        for l in range(j + 1, SUB):
            ur = spread(real_cols[l], j)
            ui = spread(imag_cols[l], j)
            real_cols[l] = real_cols[l] - (sr * ur - si * ui)
            imag_cols[l] = imag_cols[l] - (sr * ui + si * ur)
        one = spread(rows, j)
        two = spread(turned, j)
        rows = rows - (sr * one + si * two)
        turned = turned - (sr * two - si * one)
    return rows * scale, turned * scale


def invert_block(tiles, lane, sub, sign):
    count = len(tiles)
    for t in range(count):
        k = SUB * t
        in_re = (lane >= k) & (lane < k + SUB)
        in_im = (lane >= HALF + k) & (lane < HALF + k + SUB)
        inside = in_re | in_im
        real_cols = [lane_spread(tiles[t], k + l) for l in range(SUB)]
        imag_cols = [lane_spread(tiles[t], HALF + k + l) for l in range(SUB)]
        unit = jnp.where(in_re & (lane - k == sub), 1.0, 0.0)
        rows = jnp.where(inside, unit, tiles[t])
        turned = pltpu.roll(rows, HALF, 1) * sign
        rows, turned = invert_rows(real_cols, imag_cols, rows, turned, sub)
        ones = [spread(rows, l) for l in range(SUB)]
        twos = [spread(turned, l) for l in range(SUB)]
        fresh = list(tiles)
        fresh[t] = rows
        for i in list(range(t + 1, count)) + list(range(t)):
            terms = []
            for l in range(SUB):
                cr = lane_spread(tiles[i], k + l)
                ci = lane_spread(tiles[i], HALF + k + l)
                terms.append(cr * ones[l] + ci * twos[l])
            fresh[i] = jnp.where(inside, 0.0, tiles[i]) - tree_sum(terms)
        tiles = fresh
    return tiles


def turn(value, sign):
    tiles = value.shape[1] // LANES
    out = [
        pltpu.roll(value[:, t * LANES : (t + 1) * LANES], HALF, 1) * sign[: value.shape[0]]
        for t in range(tiles)
    ]
    return out[0] if tiles == 1 else jnp.concatenate(out, 1)


def exact_dot(a, b):
    return jnp.dot(a, b, precision=HIGH, preferred_element_type=jnp.float32)


def solve_kernel(train_count, beams, gram_ref, steer_ref, spec_ref, out_ref, mat, xs):
    blocks = gram_ref.shape[0] // LANES
    lane = lax.broadcasted_iota(jnp.int32, (SUB, LANES), 1)
    sub = lax.broadcasted_iota(jnp.int32, (SUB, LANES), 0)
    sign = jnp.where(lane < HALF, -1.0, 1.0)
    blane = lax.broadcasted_iota(jnp.int32, (HALF, LANES), 1)
    brow = lax.broadcasted_iota(jnp.int32, (HALF, LANES), 0)
    bsign = jnp.where(blane < HALF, -1.0, 1.0)
    inv = 1.0 / train_count
    diag = blane == brow
    trace = jnp.zeros((HALF, LANES), jnp.float32)
    for i in range(blocks):
        for j in range(blocks):
            top = gram_ref[i * LANES : i * LANES + HALF, j * LANES : (j + 1) * LANES]
            low = gram_ref[i * LANES + HALF : (i + 1) * LANES, j * LANES : (j + 1) * LANES]
            value = (pltpu.roll(low, HALF, 1) - top * bsign) * inv
            mat[i * HALF : (i + 1) * HALF, j * LANES : (j + 1) * LANES] = value
            if i == j:
                trace = trace + jnp.where(diag, value, 0.0)
        mat[i * HALF : (i + 1) * HALF, blocks * LANES :] = steer_ref[i * HALF : (i + 1) * HALF, :]
    load = LOAD_EPS * jnp.sum(trace, keepdims=True) / (blocks * HALF)
    for i in range(blocks):
        at = (slice(i * HALF, (i + 1) * HALF), slice(i * LANES, (i + 1) * LANES))
        mat[at] = mat[at] + jnp.where(diag, load, 0.0)

    norm = jnp.zeros((HALF, LANES), jnp.float32)
    for k in range(blocks):
        rows = slice(k * HALF, (k + 1) * HALF)
        tiles = [
            mat[k * HALF + SUB * t : k * HALF + SUB * (t + 1), k * LANES : (k + 1) * LANES]
            for t in range(HALF // SUB)
        ]
        inverse = jnp.concatenate(invert_block(tiles, lane, sub, sign), 0)
        right = mat[rows, (k + 1) * LANES :]
        upper = exact_dot(inverse, jnp.concatenate([right, turn(right, bsign)], 0))
        norm = norm + right[:, -LANES:] * upper[:, -LANES:]
        mat[rows, (k + 1) * LANES :] = upper
        if k + 1 < blocks:
            below = slice((k + 1) * HALF, blocks * HALF)
            both = jnp.concatenate([upper, turn(upper, bsign)], 0)
            mat[below, (k + 1) * LANES :] = mat[below, (k + 1) * LANES :] - exact_dot(
                mat[below, k * LANES : (k + 1) * LANES], both
            )
    total = jnp.sum(norm, axis=0, keepdims=True)
    total = total + pltpu.roll(jnp.broadcast_to(total, (SUB, LANES)), HALF, 1)[:1]
    low8 = (blane[:1] % HALF) < beams
    factor = jnp.where(low8, lax.rsqrt(jnp.where(low8, total, 1.0)), 0.0)
    for k in reversed(range(blocks)):
        rows = slice(k * HALF, (k + 1) * HALF)
        value = mat[rows, blocks * LANES :]
        if k + 1 < blocks:
            value = value - exact_dot(
                mat[rows, (k + 1) * LANES : blocks * LANES], xs[(k + 1) * LANES : blocks * LANES, :]
            )
        xs[k * LANES : k * LANES + HALF, :] = value
        xs[k * LANES + HALF : (k + 1) * LANES, :] = turn(value, bsign)
    weights = jnp.concatenate(
        [(xs[k * LANES : k * LANES + HALF, :] * factor).astype(jnp.bfloat16) for k in range(blocks)], 0
    )
    contract = (((0,), (1,)), ((), ()))
    real = lax.dot_general(weights, spec_ref[0], contract, preferred_element_type=jnp.float32)
    imag = lax.dot_general(weights, spec_ref[1], contract, preferred_element_type=jnp.float32)
    out_ref[0] = real[:beams] + imag[HALF : HALF + beams]
    out_ref[1] = real[HALF : HALF + beams] - imag[:beams]


def solve_and_filter(gram, steer, spectrum, train_count, beams):
    channels = gram.shape[0] // 2
    gates = spectrum.shape[1]
    return pl.pallas_call(
        lambda *refs: solve_kernel(train_count, beams, *refs),
        out_shape=jax.ShapeDtypeStruct((2, beams, gates), jnp.float32),
        scratch_shapes=[
            pltpu.VMEM((channels, 2 * channels + LANES), jnp.float32),
            pltpu.VMEM((2 * channels, LANES), jnp.float32),
        ],
        name="solve_and_filter",
    )(gram, steer, spectrum)


def packed_steering(look_row, channels, angle_count):
    beams = look_row.shape[0]
    slope = 2 * look_row + 1 - angle_count
    half = jnp.pad(slope, (0, HALF - beams))
    lane = jnp.arange(LANES, dtype=jnp.int32)
    channel = jnp.arange(channels, dtype=jnp.int32)
    index = channel[:, None] * jnp.concatenate([half, half])[None, :]
    index = (index - jnp.where(lane >= HALF, angle_count // 2, 0)[None, :]) % (2 * angle_count)
    value = jnp.cos(index.astype(jnp.float32) * (math.pi / angle_count))
    return jnp.where((lane % HALF < beams)[None, :], value, 0.0)


def shift_pairs(count, stride, extent, hop):
    pairs = []
    for i in range(count):
        digit = i // stride % extent
        pairs.append((i, i + ((digit + hop) % extent - digit) * stride))
    return pairs


def gather_rows(rows, count):
    if count % 4:
        return (lax.all_gather(rows, "rng", axis=0, tiled=True),)
    outer = count // 4
    pieces = [rows]
    for hop in range(1, outer):
        pieces.append(lax.ppermute(rows, "rng", shift_pairs(count, 4, outer, hop)))
    across = [lax.ppermute(piece, "rng", shift_pairs(count, 2, 2, 1)) for piece in pieces]
    side = jnp.concatenate(pieces + across, 0)
    return side, lax.ppermute(side, "rng", shift_pairs(count, 1, 2, 1))


def on_device(radar_cube, train_gates, look_angles):
    dop = lax.axis_size("dop")
    rng = lax.axis_size("rng")
    local = radar_cube.shape[1]
    pulses = local * dop
    channels = radar_cube.shape[3]
    beams = look_angles.shape[1]
    classes = dop if local % dop == 0 else local
    parts = partial_spectra(radar_cube, doppler_table(dop, pulses), classes, dop)
    mine = [parts[0]]
    for hop in range(1, dop):
        pairs = [(d, (d + hop) % dop) for d in range(dop)]
        mine.append(lax.ppermute(parts[hop], "dop", pairs))
    spectrum, packed = finish_spectra(train_gates, mine, 1.0 / math.sqrt(pulses))
    gram = None
    for side in gather_rows(packed, rng):
        term = lax.dot_general(
            side, side, (((0,), (0,)), ((), ())), preferred_element_type=jnp.float32
        )
        gram = term if gram is None else gram + term
    steer = packed_steering(look_angles[0], channels, NANG)
    out = solve_and_filter(gram, steer, spectrum, train_gates.shape[1] * rng, beams)
    return out[:, None]


def solution(mesh):
    placed = (P(None, "dop", "rng", None), P("dop", "rng"), P("dop", None))
    return jax.shard_map(
        on_device,
        mesh=mesh,
        in_specs=placed,
        out_specs=P(None, "dop", None, "rng"),
        check_vma=False,
    )
```

```python
import math

import jax
import jax.numpy as jnp
import numpy as np
from jax import lax
from jax.experimental import pallas as pl
from jax.experimental.pallas import tpu as pltpu
from jax.sharding import PartitionSpec as P

NANG = 256
LOAD_EPS = 1e-05
HALF = 64
LANES = 128
SUB = 8
HIGH = lax.Precision.HIGHEST


def doppler_table(bin_count, pulses):
    phase = (np.arange(bin_count)[:, None] * (pulses // bin_count) * np.arange(pulses)[None, :] % pulses) * (
        2.0 * math.pi / pulses
    )
    cosine = np.cos(phase).astype(np.float32).astype(jnp.bfloat16).astype(np.float32)
    sine = np.sin(phase).astype(np.float32).astype(jnp.bfloat16).astype(np.float32)
    upper = np.stack([cosine, sine], 1)
    lower = np.stack([-sine, cosine], 1)
    return np.stack([upper, lower], 0)


def pick(values, index):
    if all(v == values[0] for v in values):
        return float(values[0])
    out = jnp.float32(values[0])
    for i, v in enumerate(values[1:], 1):
        out = jnp.where(index == i, jnp.float32(v), out)
    return out


def partial_kernel(classes, dop, table, *refs):
    cube_ref, *out_refs = refs
    me = lax.axis_index("dop")
    local, _, width = cube_ref.shape[1:]
    for base in range(0, width, LANES):
        cols = slice(base, base + LANES)
        folded = []
        for part in range(2):
            for cls in range(classes):
                total = cube_ref[part, cls, :, cols].astype(jnp.float32)
                for pulse in range(cls + classes, local, classes):
                    total = total + cube_ref[part, pulse, :, cols].astype(jnp.float32)
                folded.append(total)
        for slot, out_ref in enumerate(out_refs):
            for row in range(2):
                acc = None
                for part in range(2):
                    for cls in range(classes):
                        options = [
                            table[row, (d + slot) % dop, part, d * local + cls] for d in range(dop)
                        ]
                        term = folded[part * classes + cls] * pick(options, me)
                        acc = term if acc is None else acc + term
                out_ref[row, :, cols] = acc


def partial_spectra(cube, table, classes, dop):
    _, local, gates, channels = cube.shape
    step = 16
    return pl.pallas_call(
        lambda *refs: partial_kernel(classes, dop, table, *refs),
        grid=(gates // step,),
        in_specs=[pl.BlockSpec((2, local, step, channels), lambda i: (0, 0, i, 0))],
        out_specs=[pl.BlockSpec((2, step, channels), lambda i: (0, i, 0))] * dop,
        out_shape=[jax.ShapeDtypeStruct((2, gates, channels), jnp.float32)] * dop,
        name="partial_spectra",
    )(cube)


def finish_kernel(scale, *refs):
    gates_ref, *parts, spec_ref, pack_ref = refs
    train = gates_ref.shape[1]
    gates = spec_ref.shape[1]
    shift = gates - train
    index = lax.broadcasted_iota(jnp.int32, (1, train), 1)
    same = jnp.where(gates_ref[...] == index, 1.0, 0.0)
    start = jnp.sum(same, axis=1, keepdims=True)
    row = lax.broadcasted_iota(jnp.int32, (train, LANES), 0).astype(jnp.float32)
    early = row < start
    lane = lax.broadcasted_iota(jnp.int32, (train, LANES), 1)
    low = lane < HALF
    for tile in range(spec_ref.shape[2] // LANES):
        cols = slice(tile * LANES, (tile + 1) * LANES)
        picked = []
        for part in range(2):
            total = parts[0][part, :, cols]
            for other in parts[1:]:
                total = total + other[part, :, cols]
            value = (total * scale).astype(jnp.bfloat16)
            spec_ref[part, :, cols] = value
            value = value.astype(jnp.float32)
            picked.append(jnp.where(early, value[:train], value[shift:]))
        real, imag = picked
        first = jnp.where(low, real, pltpu.roll(imag, HALF, 1))
        second = jnp.where(low, pltpu.roll(real, HALF, 1), imag)
        base = 2 * tile * LANES
        pack_ref[:, base : base + LANES] = first.astype(jnp.bfloat16)
        pack_ref[:, base + LANES : base + 2 * LANES] = second.astype(jnp.bfloat16)


def finish_spectra(gate_row, parts, scale):
    _, gates, channels = parts[0].shape
    train = gate_row.shape[1]
    return pl.pallas_call(
        lambda *refs: finish_kernel(scale, *refs),
        out_shape=(
            jax.ShapeDtypeStruct((2, gates, channels), jnp.bfloat16),
            jax.ShapeDtypeStruct((train, 2 * channels), jnp.bfloat16),
        ),
        name="finish_spectra",
    )(gate_row, *parts)


def spread(value, row):
    return jnp.broadcast_to(value[row : row + 1, :], (SUB, LANES))


def lane_spread(value, index, lane):
    kept = jnp.where(lane == index, value, 0.0)
    return jnp.broadcast_to(jnp.sum(kept, axis=1, keepdims=True), (SUB, LANES))


def tree_sum(terms):
    terms = list(terms)
    while len(terms) > 1:
        nxt = [terms[i] + terms[i + 1] for i in range(0, len(terms) - 1, 2)]
        if len(terms) % 2:
            nxt.append(terms[-1])
        terms = nxt
    return terms[0]


def invert_rows(real_cols, imag_cols, rows, turned, sub):
    recip = 1.0 / spread(real_cols[0], 0)
    scale = recip
    for j in range(SUB):
        own = sub == j
        if j:
            scale = jnp.where(own, recip, scale)
        cr = jnp.where(own, 0.0, real_cols[j])
        ci = jnp.where(own, 0.0, imag_cols[j])
        following = None
        if j + 1 < SUB:
            ur = spread(real_cols[j + 1], j)
            ui = spread(imag_cols[j + 1], j)
            real_cols[j + 1] = real_cols[j + 1] - (cr * ur - ci * ui) * recip
            imag_cols[j + 1] = imag_cols[j + 1] - (cr * ui + ci * ur) * recip
            following = 1.0 / spread(real_cols[j + 1], j + 1)
        sr = cr * recip
        si = ci * recip
        for l in range(j + 2, SUB):
            ur = spread(real_cols[l], j)
            ui = spread(imag_cols[l], j)
            real_cols[l] = real_cols[l] - (sr * ur - si * ui)
            imag_cols[l] = imag_cols[l] - (sr * ui + si * ur)
        one = spread(rows, j)
        two = spread(turned, j)
        rows = rows - (sr * one + si * two)
        turned = turned - (sr * two - si * one)
        recip = following
    return rows * scale, turned * scale


def invert_block(tiles, lane, sub, sign, hook):
    count = len(tiles)
    for t in range(count):
        k = SUB * t
        in_re = (lane >= k) & (lane < k + SUB)
        in_im = (lane >= HALF + k) & (lane < HALF + k + SUB)
        inside = in_re | in_im
        real_cols, imag_cols = [], []
        for l in range(SUB):
            real_cols.append(lane_spread(tiles[t], k + l, lane))
            imag_cols.append(lane_spread(tiles[t], HALF + k + l, lane))
        unit = jnp.where(in_re & (lane - k == sub), 1.0, 0.0)
        rows = jnp.where(inside, unit, tiles[t])
        turned = pltpu.roll(rows, HALF, 1) * sign
        rows, turned = invert_rows(real_cols, imag_cols, rows, turned, sub)
        ones = [spread(rows, l) for l in range(SUB)]
        twos = [spread(turned, l) for l in range(SUB)]
        fresh = list(tiles)
        fresh[t] = rows
        for i in list(range(t + 1, count)) + list(range(t)):
            terms = []
            for l in range(SUB):
                cr = lane_spread(tiles[i], k + l, lane)
                ci = lane_spread(tiles[i], HALF + k + l, lane)
                terms.append(cr * ones[l] + ci * twos[l])
            fresh[i] = jnp.where(inside, 0.0, tiles[i]) - tree_sum(terms)
        tiles = fresh
        hook(t)
    return tiles


def turn(value, sign):
    tiles = value.shape[1] // LANES
    out = [
        pltpu.roll(value[:, t * LANES : (t + 1) * LANES], HALF, 1) * sign[: value.shape[0]]
        for t in range(tiles)
    ]
    return out[0] if tiles == 1 else jnp.concatenate(out, 1)


def exact_dot(a, b):
    return jnp.dot(a, b, precision=HIGH, preferred_element_type=jnp.float32)


def three(value):
    high = value.astype(jnp.bfloat16)
    rest = value - high.astype(jnp.float32)
    mid = rest.astype(jnp.bfloat16)
    return high, mid, (rest - mid.astype(jnp.float32)).astype(jnp.bfloat16)


def solve_kernel(train_count, beams, steer_ref, spec_ref, *refs):
    *side_refs, out_ref, mat, left6, right6, next6, under = refs
    blocks = mat.shape[0] // HALF
    lane = lax.broadcasted_iota(jnp.int32, (SUB, LANES), 1)
    sub = lax.broadcasted_iota(jnp.int32, (SUB, LANES), 0)
    sign = jnp.where(lane < HALF, -1.0, 1.0)
    blane = lax.broadcasted_iota(jnp.int32, (HALF, LANES), 1)
    brow = lax.broadcasted_iota(jnp.int32, (HALF, LANES), 0)
    bsign = jnp.where(blane < HALF, -1.0, 1.0)
    inv = 1.0 / train_count
    diag = blane == brow
    trace = jnp.zeros((HALF, LANES), jnp.float32)
    contract = (((0,), (0,)), ((), ()))
    for i in range(blocks):
        gram = None
        for side in side_refs:
            term = lax.dot_general(
                side[:, i * LANES : (i + 1) * LANES], side[...], contract, preferred_element_type=jnp.float32
            )
            gram = term if gram is None else gram + term
        for j in range(blocks):
            tile = gram[:, j * LANES : (j + 1) * LANES]
            value = (pltpu.roll(tile[HALF:], HALF, 1) - tile[:HALF] * bsign) * inv
            mat[i * HALF : (i + 1) * HALF, j * LANES : (j + 1) * LANES] = value
            if i == j:
                trace = trace + jnp.where(diag, value, 0.0)
        mat[i * HALF : (i + 1) * HALF, blocks * LANES :] = steer_ref[i * HALF : (i + 1) * HALF, :]
    load = LOAD_EPS * jnp.sum(trace, keepdims=True) / (blocks * HALF)
    for i in range(blocks):
        at = (slice(i * HALF, (i + 1) * HALF), slice(i * LANES, (i + 1) * LANES))
        mat[at] = mat[at] + jnp.where(diag, load, 0.0)

    norms = []
    pivot = mat[0:HALF, 0:LANES]
    ahead = {}
    jobs = [lambda: prepare(0)]

    def prepare(k):
        start = (k + 1) * LANES
        tile = mat[k * HALF : (k + 1) * HALF, start : start + LANES]
        turned = turn(tile, bsign)
        wide = jnp.concatenate(
            [jnp.concatenate([tile, turned], 1), jnp.concatenate([turned, -tile], 1)], 0
        )
        high, mid, low = three(wide)
        for place, part in enumerate((high, high, mid, mid, low, high)):
            next6[place * LANES : (place + 1) * LANES, :] = part
        if k + 1 < blocks:
            high, mid, low = three(mat[(k + 1) * HALF : (k + 2) * HALF, k * LANES : start])
            for place, part in enumerate((high, mid, high, low)):
                under[:, place * LANES : (place + 1) * LANES] = part

    def split_left(k, inverse):
        whole = jnp.concatenate([inverse, turn(inverse, bsign)], 0)
        scaled = exact_dot(mat[:, k * LANES : (k + 1) * LANES], whole)
        pieces = [scaled[: k * HALF], inverse, scaled[(k + 1) * HALF :]]
        scaled = jnp.concatenate(pieces if k else pieces[1:], 0)
        high, mid, low = three(scaled)
        for place, part in enumerate((high, mid, high, mid, high, low)):
            left6[:, place * LANES : (place + 1) * LANES] = part

    def split_right(k, tile):
        at = slice(tile * LANES, (tile + 1) * LANES)
        right = mat[k * HALF : (k + 1) * HALF, at]
        high, mid, low = three(jnp.concatenate([right, turn(right, bsign)], 0))
        for place, part in enumerate((high, high, mid, mid, low, high)):
            right6[place * LANES : (place + 1) * LANES, at] = part

    def update(k, tile, count):
        own = slice(k * HALF, (k + 1) * HALF)
        at = slice(tile * LANES, (tile + count) * LANES)
        change = jnp.dot(left6[...], right6[:, at], preferred_element_type=jnp.float32)
        if tile + count > blocks:
            norms.append(mat[own, blocks * LANES :] * change[own, -LANES:])
        if k:
            mat[: k * HALF, at] = mat[: k * HALF, at] - change[: k * HALF]
        mat[own, at] = change[own]
        below = slice((k + 1) * HALF, None)
        mat[below, at] = mat[below, at] - change[below]

    def packed_dot(pairs):
        out = None
        for a, b in pairs:
            term = jnp.dot(a, b, preferred_element_type=jnp.float32)
            out = term if out is None else out + term
        return out

    for k in range(blocks):
        tiles = [pivot[SUB * t : SUB * (t + 1)] for t in range(HALF // SUB)]
        panels = HALF // SUB

        def hook(t, jobs=jobs):
            for job in jobs[t * len(jobs) // panels : (t + 1) * len(jobs) // panels]:
                job()

        inverse = jnp.concatenate(invert_block(tiles, lane, sub, sign, hook), 0)
        start = (k + 1) * LANES
        high, mid, low = three(inverse)
        upper = jnp.concatenate([high, mid], 1)
        lower = jnp.concatenate([high, low], 1)
        first = packed_dot(
            [
                (upper, next6[0 : 2 * LANES, :]),
                (upper, next6[2 * LANES : 4 * LANES, :]),
                (lower, next6[4 * LANES :, :]),
            ]
        )
        if k + 1 < blocks:
            high, mid, low = three(jnp.concatenate([first[:, :LANES], first[:, LANES:]], 0))
            wide = jnp.concatenate([high, mid], 1)
            change = jnp.dot(
                under[:, : 2 * LANES], jnp.concatenate([wide, wide], 0), preferred_element_type=jnp.float32
            )
            change = change[:, :LANES] + change[:, LANES:]
            change = change + jnp.dot(
                under[:, 2 * LANES :], jnp.concatenate([low, high], 0), preferred_element_type=jnp.float32
            )
            pivot = mat[(k + 1) * HALF : (k + 2) * HALF, start : start + LANES] - change
            jobs = [lambda k=k, inverse=inverse: split_left(k, inverse)]
            for j in range(k + 1, blocks + 1, 2):
                count = min(2, blocks + 1 - j)
                for c in range(count):
                    jobs.append(lambda k=k, j=j, c=c: split_right(k, j + c))
                jobs.append(lambda k=k, j=j, count=count: update(k, j, count))
            jobs.append(lambda k=k: prepare(k + 1))
        else:
            own = slice(k * HALF, (k + 1) * HALF)
            norms.append(mat[own, start:] * first[:, :LANES])
            mat[own, start:] = first[:, :LANES]
            both = jnp.concatenate([first[:, :LANES], first[:, LANES:]], 0)
            above = slice(0, k * HALF)
            mat[above, start:] = mat[above, start:] - exact_dot(mat[above, k * LANES : start], both)
    norm = tree_sum(norms)
    total = jnp.sum(norm, axis=0, keepdims=True)
    total = total + pltpu.roll(jnp.broadcast_to(total, (SUB, LANES)), HALF, 1)[:1]
    low8 = (blane[:1] % HALF) < beams
    factor = jnp.where(low8, lax.rsqrt(jnp.where(low8, total, 1.0)), 0.0)
    weights = (mat[:, blocks * LANES :] * factor).astype(jnp.bfloat16)
    contract = (((0,), (1,)), ((), ()))
    real = lax.dot_general(weights, spec_ref[0], contract, preferred_element_type=jnp.float32)
    imag = lax.dot_general(weights, spec_ref[1], contract, preferred_element_type=jnp.float32)
    out_ref[0] = real[:beams] + imag[HALF : HALF + beams]
    out_ref[1] = real[HALF : HALF + beams] - imag[:beams]


def solve_and_filter(sides, steer, spectrum, train_count, beams):
    channels = sides[0].shape[1] // 2
    gates = spectrum.shape[1]
    width = 2 * channels + LANES
    return pl.pallas_call(
        lambda *refs: solve_kernel(train_count, beams, *refs),
        out_shape=jax.ShapeDtypeStruct((2, beams, gates), jnp.float32),
        scratch_shapes=[
            pltpu.VMEM((channels, width), jnp.float32),
            pltpu.VMEM((channels, 6 * LANES), jnp.bfloat16),
            pltpu.VMEM((6 * LANES, width), jnp.bfloat16),
            pltpu.VMEM((6 * LANES, 2 * LANES), jnp.bfloat16),
            pltpu.VMEM((HALF, 4 * LANES), jnp.bfloat16),
        ],
        name="solve_and_filter",
    )(steer, spectrum, *sides)


def packed_steering(look_row, channels, angle_count):
    beams = look_row.shape[0]
    slope = 2 * look_row + 1 - angle_count
    half = jnp.pad(slope, (0, HALF - beams))
    lane = jnp.arange(LANES, dtype=jnp.int32)
    channel = jnp.arange(channels, dtype=jnp.int32)
    index = channel[:, None] * jnp.concatenate([half, half])[None, :]
    index = (index - jnp.where(lane >= HALF, angle_count // 2, 0)[None, :]) % (2 * angle_count)
    value = jnp.cos(index.astype(jnp.float32) * (math.pi / angle_count))
    return jnp.where((lane % HALF < beams)[None, :], value, 0.0)


def shift_pairs(count, stride, extent, hop):
    pairs = []
    for i in range(count):
        digit = i // stride % extent
        pairs.append((i, i + ((digit + hop) % extent - digit) * stride))
    return pairs


def gather_rows(rows, count):
    if count % 4:
        return (lax.all_gather(rows, "rng", axis=0, tiled=True),)
    outer = count // 4
    pieces = [rows]
    for hop in range(1, outer):
        pieces.append(lax.ppermute(rows, "rng", shift_pairs(count, 4, outer, hop)))
    across = [lax.ppermute(piece, "rng", shift_pairs(count, 2, 2, 1)) for piece in pieces]
    side = jnp.concatenate(pieces + across, 0)
    return side, lax.ppermute(side, "rng", shift_pairs(count, 1, 2, 1))


def on_device(radar_cube, train_gates, look_angles):
    dop = lax.axis_size("dop")
    rng = lax.axis_size("rng")
    local = radar_cube.shape[1]
    pulses = local * dop
    channels = radar_cube.shape[3]
    beams = look_angles.shape[1]
    classes = dop if local % dop == 0 else local
    parts = partial_spectra(radar_cube, doppler_table(dop, pulses), classes, dop)
    mine = [parts[0]]
    for hop in range(1, dop):
        pairs = [(d, (d + hop) % dop) for d in range(dop)]
        mine.append(lax.ppermute(parts[hop], "dop", pairs))
    spectrum, packed = finish_spectra(train_gates, mine, 1.0 / math.sqrt(pulses))
    sides = gather_rows(packed, rng)
    steer = packed_steering(look_angles[0], channels, NANG)
    out = solve_and_filter(sides, steer, spectrum, train_gates.shape[1] * rng, beams)
    return out[:, None]


def solution(mesh):
    placed = (P(None, "dop", "rng", None), P("dop", "rng"), P("dop", None))
    return jax.shard_map(
        on_device,
        mesh=mesh,
        in_specs=placed,
        out_specs=P(None, "dop", None, "rng"),
        check_vma=False,
    )
```

```python
import math

import jax
import jax.numpy as jnp
import numpy as np
from jax import lax
from jax.experimental import pallas as pl
from jax.experimental.pallas import tpu as pltpu
from jax.sharding import PartitionSpec as P

NANG = 256
LOAD_EPS = 1e-05
HALF = 64
LANES = 128
SUB = 8
HIGH = lax.Precision.HIGHEST


def doppler_table(bin_count, pulses):
    phase = (np.arange(bin_count)[:, None] * (pulses // bin_count) * np.arange(pulses)[None, :] % pulses) * (
        2.0 * math.pi / pulses
    )
    cosine = np.cos(phase).astype(np.float32).astype(jnp.bfloat16).astype(np.float32)
    sine = np.sin(phase).astype(np.float32).astype(jnp.bfloat16).astype(np.float32)
    upper = np.stack([cosine, sine], 1)
    lower = np.stack([-sine, cosine], 1)
    return np.stack([upper, lower], 0)


def pick(values, index):
    if all(v == values[0] for v in values):
        return float(values[0])
    out = jnp.float32(values[0])
    for i, v in enumerate(values[1:], 1):
        out = jnp.where(index == i, jnp.float32(v), out)
    return out


def partial_kernel(classes, dop, table, *refs):
    cube_ref, *out_refs, buf, sems = refs
    me = lax.axis_index("dop")
    steps, _, local, step, width = buf.shape

    def copy(n):
        rows = pl.ds(pl.multiple_of(n * step, step), step)
        return pltpu.make_async_copy(cube_ref.at[:, :, rows, :], buf.at[n], sems.at[n])

    for n in range(steps):
        copy(n).start()

    def body(n, carry):
        copy(n).wait()
        rows = pl.ds(pl.multiple_of(n * step, step), step)
        for base in range(0, width, LANES):
            cols = slice(base, base + LANES)
            folded = []
            for part in range(2):
                for cls in range(classes):
                    total = buf[n, part, cls, :, cols].astype(jnp.float32)
                    for pulse in range(cls + classes, local, classes):
                        total = total + buf[n, part, pulse, :, cols].astype(jnp.float32)
                    folded.append(total)
            for slot, out_ref in enumerate(out_refs):
                for row in range(2):
                    acc = None
                    for part in range(2):
                        for cls in range(classes):
                            options = [
                                table[row, (d + slot) % dop, part, d * local + cls] for d in range(dop)
                            ]
                            term = folded[part * classes + cls] * pick(options, me)
                            acc = term if acc is None else acc + term
                    out_ref[row, rows, cols] = acc.astype(out_ref.dtype)
        return carry

    lax.fori_loop(0, steps, body, 0)


def partial_spectra(cube, table, classes, dop):
    _, local, gates, channels = cube.shape
    step = 16
    steps = gates // step
    return pl.pallas_call(
        lambda *refs: partial_kernel(classes, dop, table, *refs),
        in_specs=[pl.BlockSpec(memory_space=pltpu.HBM)],
        out_specs=[pl.BlockSpec(memory_space=pltpu.VMEM)] * dop,
        out_shape=[jax.ShapeDtypeStruct((2, gates, channels), jnp.float32)] * dop,
        scratch_shapes=[
            pltpu.VMEM((steps, 2, local, step, channels), cube.dtype),
            pltpu.SemaphoreType.DMA((steps,)),
        ],
        compiler_params=pltpu.CompilerParams(vmem_limit_bytes=52 << 20),
        name="partial_spectra",
    )(cube)


def finish_kernel(scale, *refs):
    gates_ref, *parts, spec_ref, pack_ref = refs
    train = gates_ref.shape[1]
    gates = spec_ref.shape[1]
    shift = gates - train
    index = lax.broadcasted_iota(jnp.int32, (1, train), 1)
    same = jnp.where(gates_ref[...] == index, 1.0, 0.0)
    start = jnp.sum(same, axis=1, keepdims=True)
    row = lax.broadcasted_iota(jnp.int32, (train, LANES), 0).astype(jnp.float32)
    early = row < start
    lane = lax.broadcasted_iota(jnp.int32, (train, LANES), 1)
    low = lane < HALF
    for tile in range(spec_ref.shape[2] // LANES):
        cols = slice(tile * LANES, (tile + 1) * LANES)
        picked = []
        for part in range(2):
            total = parts[0][part, :, cols]
            for other in parts[1:]:
                total = total + other[part, :, cols]
            value = (total * scale).astype(jnp.bfloat16)
            spec_ref[part, :, cols] = value
            value = value.astype(jnp.float32)
            picked.append(jnp.where(early, value[:train], value[shift:]))
        real, imag = picked
        first = jnp.where(low, real, pltpu.roll(imag, HALF, 1))
        second = jnp.where(low, pltpu.roll(real, HALF, 1), imag)
        base = 2 * tile * LANES
        pack_ref[:, base : base + LANES] = first.astype(jnp.bfloat16)
        pack_ref[:, base + LANES : base + 2 * LANES] = second.astype(jnp.bfloat16)


def finish_spectra(gate_row, parts, scale):
    _, gates, channels = parts[0].shape
    train = gate_row.shape[1]
    return pl.pallas_call(
        lambda *refs: finish_kernel(scale, *refs),
        out_shape=(
            jax.ShapeDtypeStruct((2, gates, channels), jnp.bfloat16),
            jax.ShapeDtypeStruct((train, 2 * channels), jnp.bfloat16),
        ),
        in_specs=[pl.BlockSpec(memory_space=pltpu.VMEM)] * (1 + len(parts)),
        out_specs=[pl.BlockSpec(memory_space=pltpu.VMEM)] * 2,
        compiler_params=pltpu.CompilerParams(vmem_limit_bytes=8 << 20),
        name="finish_spectra",
    )(gate_row, *parts)


def spread(value, row):
    return jnp.broadcast_to(value[row : row + 1, :], (SUB, LANES))


def lane_spread(value, index, lane):
    kept = jnp.where(lane == index, value, 0.0)
    return jnp.broadcast_to(jnp.sum(kept, axis=1, keepdims=True), (SUB, LANES))


def tree_sum(terms):
    terms = list(terms)
    while len(terms) > 1:
        nxt = [terms[i] + terms[i + 1] for i in range(0, len(terms) - 1, 2)]
        if len(terms) % 2:
            nxt.append(terms[-1])
        terms = nxt
    return terms[0]


def invert_rows(real_cols, imag_cols, rows, turned, sub):
    recip = 1.0 / spread(real_cols[0], 0)
    scale = recip
    for j in range(SUB):
        own = sub == j
        if j:
            scale = jnp.where(own, recip, scale)
        cr = jnp.where(own, 0.0, real_cols[j])
        ci = jnp.where(own, 0.0, imag_cols[j])
        following = None
        if j + 1 < SUB:
            ur = spread(real_cols[j + 1], j)
            ui = spread(imag_cols[j + 1], j)
            real_cols[j + 1] = real_cols[j + 1] - (cr * ur - ci * ui) * recip
            imag_cols[j + 1] = imag_cols[j + 1] - (cr * ui + ci * ur) * recip
            following = 1.0 / spread(real_cols[j + 1], j + 1)
        sr = cr * recip
        si = ci * recip
        for l in range(j + 2, SUB):
            ur = spread(real_cols[l], j)
            ui = spread(imag_cols[l], j)
            real_cols[l] = real_cols[l] - (sr * ur - si * ui)
            imag_cols[l] = imag_cols[l] - (sr * ui + si * ur)
        one = spread(rows, j)
        two = spread(turned, j)
        rows = rows - (sr * one + si * two)
        turned = turned - (sr * two - si * one)
        recip = following
    return rows * scale, turned * scale


def invert_block(tiles, lane, sub, sign, hook):
    count = len(tiles)
    for t in range(count):
        k = SUB * t
        in_re = (lane >= k) & (lane < k + SUB)
        in_im = (lane >= HALF + k) & (lane < HALF + k + SUB)
        inside = in_re | in_im
        real_cols, imag_cols = [], []
        for l in range(SUB):
            real_cols.append(lane_spread(tiles[t], k + l, lane))
            imag_cols.append(lane_spread(tiles[t], HALF + k + l, lane))
        unit = jnp.where(in_re & (lane - k == sub), 1.0, 0.0)
        rows = jnp.where(inside, unit, tiles[t])
        turned = pltpu.roll(rows, HALF, 1) * sign
        rows, turned = invert_rows(real_cols, imag_cols, rows, turned, sub)
        ones = [spread(rows, l) for l in range(SUB)]
        twos = [spread(turned, l) for l in range(SUB)]
        fresh = list(tiles)
        fresh[t] = rows
        for i in list(range(t + 1, count)) + list(range(t)):
            terms = []
            for l in range(SUB):
                cr = lane_spread(tiles[i], k + l, lane)
                ci = lane_spread(tiles[i], HALF + k + l, lane)
                terms.append(cr * ones[l] + ci * twos[l])
            fresh[i] = jnp.where(inside, 0.0, tiles[i]) - tree_sum(terms)
        tiles = fresh
        hook(t)
    return tiles


def turn(value, sign):
    tiles = value.shape[1] // LANES
    out = [
        pltpu.roll(value[:, t * LANES : (t + 1) * LANES], HALF, 1) * sign[: value.shape[0]]
        for t in range(tiles)
    ]
    return out[0] if tiles == 1 else jnp.concatenate(out, 1)


def exact_dot(a, b):
    return jnp.dot(a, b, precision=HIGH, preferred_element_type=jnp.float32)


def three(value):
    high = value.astype(jnp.bfloat16)
    rest = value - high.astype(jnp.float32)
    mid = rest.astype(jnp.bfloat16)
    return high, mid, (rest - mid.astype(jnp.float32)).astype(jnp.bfloat16)


def solve_kernel(train_count, beams, steer_ref, spec_ref, *refs):
    *side_refs, out_ref, mat, left6, right6, next6, under = refs
    blocks = mat.shape[0] // HALF
    lane = lax.broadcasted_iota(jnp.int32, (SUB, LANES), 1)
    sub = lax.broadcasted_iota(jnp.int32, (SUB, LANES), 0)
    sign = jnp.where(lane < HALF, -1.0, 1.0)
    blane = lax.broadcasted_iota(jnp.int32, (HALF, LANES), 1)
    brow = lax.broadcasted_iota(jnp.int32, (HALF, LANES), 0)
    bsign = jnp.where(blane < HALF, -1.0, 1.0)
    inv = 1.0 / train_count
    diag = blane == brow
    trace = jnp.zeros((HALF, LANES), jnp.float32)
    contract = (((0,), (0,)), ((), ()))
    for i in range(blocks):
        gram = None
        for side in side_refs:
            term = lax.dot_general(
                side[:, i * LANES : (i + 1) * LANES], side[...], contract, preferred_element_type=jnp.float32
            )
            gram = term if gram is None else gram + term
        for j in range(blocks):
            tile = gram[:, j * LANES : (j + 1) * LANES]
            value = (pltpu.roll(tile[HALF:], HALF, 1) - tile[:HALF] * bsign) * inv
            mat[i * HALF : (i + 1) * HALF, j * LANES : (j + 1) * LANES] = value
            if i == j:
                trace = trace + jnp.where(diag, value, 0.0)
        mat[i * HALF : (i + 1) * HALF, blocks * LANES :] = steer_ref[i * HALF : (i + 1) * HALF, :]
    load = LOAD_EPS * jnp.sum(trace, keepdims=True) / (blocks * HALF)
    for i in range(blocks):
        at = (slice(i * HALF, (i + 1) * HALF), slice(i * LANES, (i + 1) * LANES))
        mat[at] = mat[at] + jnp.where(diag, load, 0.0)

    norms = []
    pivot = mat[0:HALF, 0:LANES]
    ahead = {}
    jobs = [lambda: prepare(0)]

    def prepare(k):
        start = (k + 1) * LANES
        tile = mat[k * HALF : (k + 1) * HALF, start : start + LANES]
        turned = turn(tile, bsign)
        wide = jnp.concatenate(
            [jnp.concatenate([tile, turned], 1), jnp.concatenate([turned, -tile], 1)], 0
        )
        high, mid, low = three(wide)
        for place, part in enumerate((high, high, mid, mid, low, high)):
            next6[place * LANES : (place + 1) * LANES, :] = part
        if k + 1 < blocks:
            high, mid, low = three(mat[(k + 1) * HALF : (k + 2) * HALF, k * LANES : start])
            for place, part in enumerate((high, mid, high, low)):
                under[:, place * LANES : (place + 1) * LANES] = part

    def split_left(k, inverse):
        whole = jnp.concatenate([inverse, turn(inverse, bsign)], 0)
        scaled = exact_dot(mat[:, k * LANES : (k + 1) * LANES], whole)
        pieces = [scaled[: k * HALF], inverse, scaled[(k + 1) * HALF :]]
        scaled = jnp.concatenate(pieces if k else pieces[1:], 0)
        high, mid, low = three(scaled)
        for place, part in enumerate((high, mid, high, mid, high, low)):
            left6[:, place * LANES : (place + 1) * LANES] = part

    def split_right(k, tile):
        at = slice(tile * LANES, (tile + 1) * LANES)
        right = mat[k * HALF : (k + 1) * HALF, at]
        high, mid, low = three(jnp.concatenate([right, turn(right, bsign)], 0))
        for place, part in enumerate((high, high, mid, mid, low, high)):
            right6[place * LANES : (place + 1) * LANES, at] = part

    def update(k, tile, count):
        own = slice(k * HALF, (k + 1) * HALF)
        at = slice(tile * LANES, (tile + count) * LANES)
        change = jnp.dot(left6[...], right6[:, at], preferred_element_type=jnp.float32)
        if tile + count > blocks:
            norms.append(mat[own, blocks * LANES :] * change[own, -LANES:])
        if k:
            mat[: k * HALF, at] = mat[: k * HALF, at] - change[: k * HALF]
        mat[own, at] = change[own]
        below = slice((k + 1) * HALF, None)
        mat[below, at] = mat[below, at] - change[below]

    def packed_dot(pairs):
        out = None
        for a, b in pairs:
            term = jnp.dot(a, b, preferred_element_type=jnp.float32)
            out = term if out is None else out + term
        return out

    for k in range(blocks):
        tiles = [pivot[SUB * t : SUB * (t + 1)] for t in range(HALF // SUB)]
        panels = HALF // SUB

        def hook(t, jobs=jobs):
            for job in jobs[t * len(jobs) // panels : (t + 1) * len(jobs) // panels]:
                job()

        inverse = jnp.concatenate(invert_block(tiles, lane, sub, sign, hook), 0)
        start = (k + 1) * LANES
        high, mid, low = three(inverse)
        upper = jnp.concatenate([high, mid], 1)
        lower = jnp.concatenate([high, low], 1)
        first = packed_dot(
            [
                (upper, next6[0 : 2 * LANES, :]),
                (upper, next6[2 * LANES : 4 * LANES, :]),
                (lower, next6[4 * LANES :, :]),
            ]
        )
        if k + 1 < blocks:
            high, mid, low = three(jnp.concatenate([first[:, :LANES], first[:, LANES:]], 0))
            wide = jnp.concatenate([high, mid], 1)
            change = jnp.dot(
                under[:, : 2 * LANES], jnp.concatenate([wide, wide], 0), preferred_element_type=jnp.float32
            )
            change = change[:, :LANES] + change[:, LANES:]
            change = change + jnp.dot(
                under[:, 2 * LANES :], jnp.concatenate([low, high], 0), preferred_element_type=jnp.float32
            )
            pivot = mat[(k + 1) * HALF : (k + 2) * HALF, start : start + LANES] - change
            jobs = [lambda k=k, inverse=inverse: split_left(k, inverse)]
            for j in range(k + 1, blocks + 1, 2):
                count = min(2, blocks + 1 - j)
                for c in range(count):
                    jobs.append(lambda k=k, j=j, c=c: split_right(k, j + c))
                jobs.append(lambda k=k, j=j, count=count: update(k, j, count))
            jobs.append(lambda k=k: prepare(k + 1))
        else:
            own = slice(k * HALF, (k + 1) * HALF)
            norms.append(mat[own, start:] * first[:, :LANES])
            mat[own, start:] = first[:, :LANES]
            both = jnp.concatenate([first[:, :LANES], first[:, LANES:]], 0)
            above = slice(0, k * HALF)
            mat[above, start:] = mat[above, start:] - exact_dot(mat[above, k * LANES : start], both)
    norm = tree_sum(norms)
    total = jnp.sum(norm, axis=0, keepdims=True)
    total = total + pltpu.roll(jnp.broadcast_to(total, (SUB, LANES)), HALF, 1)[:1]
    low8 = (blane[:1] % HALF) < beams
    factor = jnp.where(low8, lax.rsqrt(jnp.where(low8, total, 1.0)), 0.0)
    weights = (mat[:, blocks * LANES :] * factor).astype(jnp.bfloat16)
    contract = (((0,), (1,)), ((), ()))
    real = lax.dot_general(weights, spec_ref[0], contract, preferred_element_type=jnp.float32)
    imag = lax.dot_general(weights, spec_ref[1], contract, preferred_element_type=jnp.float32)
    out_ref[0] = real[:beams] + imag[HALF : HALF + beams]
    out_ref[1] = real[HALF : HALF + beams] - imag[:beams]


def solve_and_filter(sides, steer, spectrum, train_count, beams):
    channels = sides[0].shape[1] // 2
    gates = spectrum.shape[1]
    width = 2 * channels + LANES
    return pl.pallas_call(
        lambda *refs: solve_kernel(train_count, beams, *refs),
        out_shape=jax.ShapeDtypeStruct((2, beams, gates), jnp.float32),
        in_specs=[pl.BlockSpec(memory_space=pltpu.VMEM)] * (2 + len(sides)),
        out_specs=pl.BlockSpec(memory_space=pltpu.VMEM),
        scratch_shapes=[
            pltpu.VMEM((channels, width), jnp.float32),
            pltpu.VMEM((channels, 6 * LANES), jnp.bfloat16),
            pltpu.VMEM((6 * LANES, width), jnp.bfloat16),
            pltpu.VMEM((6 * LANES, 2 * LANES), jnp.bfloat16),
            pltpu.VMEM((HALF, 4 * LANES), jnp.bfloat16),
        ],
        compiler_params=pltpu.CompilerParams(vmem_limit_bytes=24 << 20),
        name="solve_and_filter",
    )(steer, spectrum, *sides)


def packed_steering(look_row, channels, angle_count):
    beams = look_row.shape[0]
    slope = 2 * look_row + 1 - angle_count
    half = jnp.pad(slope, (0, HALF - beams))
    lane = jnp.arange(LANES, dtype=jnp.int32)
    channel = jnp.arange(channels, dtype=jnp.int32)
    index = channel[:, None] * jnp.concatenate([half, half])[None, :]
    index = (index - jnp.where(lane >= HALF, angle_count // 2, 0)[None, :]) % (2 * angle_count)
    value = jnp.cos(index.astype(jnp.float32) * (math.pi / angle_count))
    return jnp.where((lane % HALF < beams)[None, :], value, 0.0)


def shift_pairs(count, stride, extent, hop):
    pairs = []
    for i in range(count):
        digit = i // stride % extent
        pairs.append((i, i + ((digit + hop) % extent - digit) * stride))
    return pairs


def gather_rows(rows, count):
    if count % 4:
        return (lax.all_gather(rows, "rng", axis=0, tiled=True),)
    outer = count // 4
    swap = shift_pairs(count, 2, 2, 1)
    pair = shift_pairs(count, 1, 2, 1)
    across = [lax.ppermute(rows, "rng", swap)]
    pieces = [rows]
    for hop in sorted(range(1, outer), key=lambda h: min(h, outer - h)):
        pieces.append(lax.ppermute(rows, "rng", shift_pairs(count, 4, outer, hop)))
    across += [lax.ppermute(piece, "rng", swap) for piece in pieces[1:]]
    side = jnp.concatenate(pieces + across, 0)
    return side, lax.ppermute(side, "rng", pair)


def on_device(radar_cube, train_gates, look_angles):
    dop = lax.axis_size("dop")
    rng = lax.axis_size("rng")
    local = radar_cube.shape[1]
    pulses = local * dop
    channels = radar_cube.shape[3]
    beams = look_angles.shape[1]
    classes = dop if local % dop == 0 else local
    parts = partial_spectra(radar_cube, doppler_table(dop, pulses), classes, dop)
    mine = [parts[0]]
    for hop in range(1, dop):
        pairs = [(d, (d + hop) % dop) for d in range(dop)]
        mine.append(lax.ppermute(parts[hop], "dop", pairs))
    spectrum, packed = finish_spectra(train_gates, mine, 1.0 / math.sqrt(pulses))
    sides = gather_rows(packed, rng)
    steer = packed_steering(look_angles[0], channels, NANG)
    out = solve_and_filter(sides, steer, spectrum, train_gates.shape[1] * rng, beams)
    return out[:, None]


def solution(mesh):
    placed = (P(None, "dop", "rng", None), P("dop", "rng"), P("dop", None))
    return jax.shard_map(
        on_device,
        mesh=mesh,
        in_specs=placed,
        out_specs=P(None, "dop", None, "rng"),
        check_vma=False,
    )
```

```python
import math

import jax
import jax.numpy as jnp
import numpy as np
from jax import lax
from jax.experimental import pallas as pl
from jax.experimental.pallas import tpu as pltpu
from jax.sharding import PartitionSpec as P


NANG = 256
LOAD_EPS = 1e-05
HALF = 64
LANES = 128
SUB = 8
HIGH = lax.Precision.HIGHEST


def doppler_table(bin_count, pulses):
    phase = (np.arange(bin_count)[:, None] * (pulses // bin_count) * np.arange(pulses)[None, :] % pulses) * (
        2.0 * math.pi / pulses
    )
    cosine = np.cos(phase).astype(np.float32).astype(jnp.bfloat16).astype(np.float32)
    sine = np.sin(phase).astype(np.float32).astype(jnp.bfloat16).astype(np.float32)
    upper = np.stack([cosine, sine], 1)
    lower = np.stack([-sine, cosine], 1)
    return np.stack([upper, lower], 0)


def pick(values, index):
    if all(v == values[0] for v in values):
        return float(values[0])
    out = jnp.float32(values[0])
    for i, v in enumerate(values[1:], 1):
        out = jnp.where(index == i, jnp.float32(v), out)
    return out


def partial_kernel(classes, dop, table, *refs):
    cube_ref, *out_refs, buf, sems = refs
    me = lax.axis_index("dop")
    steps, _, local, step, width = buf.shape

    def copy(n):
        rows = pl.ds(pl.multiple_of(n * step, step), step)
        return pltpu.make_async_copy(cube_ref.at[:, :, rows, :], buf.at[n], sems.at[n])

    for n in range(steps):
        copy(n).start()

    def body(n, carry):
        copy(n).wait()
        rows = pl.ds(pl.multiple_of(n * step, step), step)
        for base in range(0, width, LANES):
            cols = slice(base, base + LANES)
            folded = []
            for part in range(2):
                for cls in range(classes):
                    total = buf[n, part, cls, :, cols].astype(jnp.float32)
                    for pulse in range(cls + classes, local, classes):
                        total = total + buf[n, part, pulse, :, cols].astype(jnp.float32)
                    folded.append(total)
            for slot, out_ref in enumerate(out_refs):
                for row in range(2):
                    acc = None
                    for part in range(2):
                        for cls in range(classes):
                            options = [
                                table[row, (d + slot) % dop, part, d * local + cls] for d in range(dop)
                            ]
                            term = folded[part * classes + cls] * pick(options, me)
                            acc = term if acc is None else acc + term
                    out_ref[row, rows, cols] = acc.astype(out_ref.dtype)
        return carry

    lax.fori_loop(0, steps, body, 0)


def partial_spectra(cube, table, classes, dop):
    _, local, gates, channels = cube.shape
    step = 16
    steps = gates // step
    return pl.pallas_call(
        lambda *refs: partial_kernel(classes, dop, table, *refs),
        in_specs=[pl.BlockSpec(memory_space=pltpu.HBM)],
        out_specs=[pl.BlockSpec(memory_space=pltpu.VMEM)] * dop,
        out_shape=[
            jax.ShapeDtypeStruct((2, gates, channels), jnp.float32)
            for _ in range(dop)
        ],
        scratch_shapes=[
            pltpu.VMEM((steps, 2, local, step, channels), cube.dtype),
            pltpu.SemaphoreType.DMA((steps,)),
        ],
        compiler_params=pltpu.CompilerParams(vmem_limit_bytes=52 << 20),
        name="partial_spectra",
    )(cube)


def finish_kernel(scale, *refs):
    gates_ref, *parts, spec_ref, pack_ref = refs
    train = gates_ref.shape[1]
    gates = spec_ref.shape[1]
    shift = gates - train
    index = lax.broadcasted_iota(jnp.int32, (1, train), 1)
    same = jnp.where(gates_ref[...] == index, 1.0, 0.0)
    start = jnp.sum(same, axis=1, keepdims=True)
    row = lax.broadcasted_iota(jnp.int32, (train, LANES), 0).astype(jnp.float32)
    early = row < start
    lane = lax.broadcasted_iota(jnp.int32, (train, LANES), 1)
    low = lane < HALF
    for tile in range(spec_ref.shape[2] // LANES):
        cols = slice(tile * LANES, (tile + 1) * LANES)
        picked = []
        for part in range(2):
            total = parts[0][part, :, cols]
            for other in parts[1:]:
                total = total + other[part, :, cols].astype(jnp.float32)
            value = (total * scale).astype(jnp.bfloat16)
            spec_ref[part, :, cols] = value
            value = value.astype(jnp.float32)
            picked.append(jnp.where(early, value[:train], value[shift:]))
        real, imag = picked
        first = jnp.where(low, real, pltpu.roll(imag, HALF, 1))
        second = jnp.where(low, pltpu.roll(real, HALF, 1), imag)
        base = 2 * tile * LANES
        pack_ref[:, base : base + LANES] = first.astype(jnp.bfloat16)
        pack_ref[:, base + LANES : base + 2 * LANES] = second.astype(jnp.bfloat16)


def finish_spectra(gate_row, parts, scale):
    _, gates, channels = parts[0].shape
    train = gate_row.shape[1]
    return pl.pallas_call(
        lambda *refs: finish_kernel(scale, *refs),
        out_shape=(
            jax.ShapeDtypeStruct((2, gates, channels), jnp.bfloat16),
            jax.ShapeDtypeStruct((train, 2 * channels), jnp.bfloat16),
        ),
        in_specs=[pl.BlockSpec(memory_space=pltpu.VMEM)] * (1 + len(parts)),
        out_specs=[pl.BlockSpec(memory_space=pltpu.VMEM)] * 2,
        compiler_params=pltpu.CompilerParams(vmem_limit_bytes=8 << 20),
        name="finish_spectra",
    )(gate_row, *parts)


def spread(value, row):
    return jnp.broadcast_to(value[row : row + 1, :], (SUB, LANES))


def lane_spread(value, index, lane):
    kept = jnp.where(lane == index, value, 0.0)
    return jnp.broadcast_to(jnp.sum(kept, axis=1, keepdims=True), (SUB, LANES))


def tree_sum(terms):
    terms = list(terms)
    while len(terms) > 1:
        nxt = [terms[i] + terms[i + 1] for i in range(0, len(terms) - 1, 2)]
        if len(terms) % 2:
            nxt.append(terms[-1])
        terms = nxt
    return terms[0]


def invert_rows(real_cols, imag_cols, rows, turned, sub):
    recip = 1.0 / spread(real_cols[0], 0)
    scale = recip
    for j in range(SUB):
        own = sub == j
        if j:
            scale = jnp.where(own, recip, scale)
        cr = jnp.where(own, 0.0, real_cols[j])
        ci = jnp.where(own, 0.0, imag_cols[j])
        following = None
        if j + 1 < SUB:
            ur = spread(real_cols[j + 1], j)
            ui = spread(imag_cols[j + 1], j)
            real_cols[j + 1] = real_cols[j + 1] - (cr * ur - ci * ui) * recip
            imag_cols[j + 1] = imag_cols[j + 1] - (cr * ui + ci * ur) * recip
            following = 1.0 / spread(real_cols[j + 1], j + 1)
        sr = cr * recip
        si = ci * recip
        for l in range(j + 2, SUB):
            ur = spread(real_cols[l], j)
            ui = spread(imag_cols[l], j)
            real_cols[l] = real_cols[l] - (sr * ur - si * ui)
            imag_cols[l] = imag_cols[l] - (sr * ui + si * ur)
        one = spread(rows, j)
        two = spread(turned, j)
        rows = rows - (sr * one + si * two)
        turned = turned - (sr * two - si * one)
        recip = following
    return rows * scale, turned * scale


def invert_block(tiles, lane, sub, sign, hook):
    count = len(tiles)
    for t in range(count):
        k = SUB * t
        in_re = (lane >= k) & (lane < k + SUB)
        in_im = (lane >= HALF + k) & (lane < HALF + k + SUB)
        inside = in_re | in_im
        real_cols, imag_cols = [], []
        for l in range(SUB):
            real_cols.append(lane_spread(tiles[t], k + l, lane))
            imag_cols.append(lane_spread(tiles[t], HALF + k + l, lane))
        unit = jnp.where(in_re & (lane - k == sub), 1.0, 0.0)
        rows = jnp.where(inside, unit, tiles[t])
        turned = pltpu.roll(rows, HALF, 1) * sign
        rows, turned = invert_rows(real_cols, imag_cols, rows, turned, sub)
        ones = [spread(rows, l) for l in range(SUB)]
        twos = [spread(turned, l) for l in range(SUB)]
        fresh = list(tiles)
        fresh[t] = rows
        for i in list(range(t + 1, count)) + list(range(t)):
            terms = []
            for l in range(SUB):
                cr = lane_spread(tiles[i], k + l, lane)
                ci = lane_spread(tiles[i], HALF + k + l, lane)
                terms.append(cr * ones[l] + ci * twos[l])
            fresh[i] = jnp.where(inside, 0.0, tiles[i]) - tree_sum(terms)
        tiles = fresh
        hook(t)
    return tiles


def turn(value, sign):
    tiles = value.shape[1] // LANES
    out = [
        pltpu.roll(value[:, t * LANES : (t + 1) * LANES], HALF, 1) * sign[: value.shape[0]]
        for t in range(tiles)
    ]
    return out[0] if tiles == 1 else jnp.concatenate(out, 1)


def exact_dot(a, b):
    return jnp.dot(a, b, precision=HIGH, preferred_element_type=jnp.float32)


def three(value):
    high = value.astype(jnp.bfloat16)
    rest = value - high.astype(jnp.float32)
    mid = rest.astype(jnp.bfloat16)
    return high, mid, (rest - mid.astype(jnp.float32)).astype(jnp.bfloat16)


def solve_kernel(train_count, beams, steer_ref, spec_ref, *refs):
    *side_refs, out_ref, mat, left6, right6, next6, under, flipped = refs
    blocks = mat.shape[0] // HALF
    lane = lax.broadcasted_iota(jnp.int32, (SUB, LANES), 1)
    sub = lax.broadcasted_iota(jnp.int32, (SUB, LANES), 0)
    sign = jnp.where(lane < HALF, -1.0, 1.0)
    blane = lax.broadcasted_iota(jnp.int32, (HALF, LANES), 1)
    brow = lax.broadcasted_iota(jnp.int32, (HALF, LANES), 0)
    bsign = jnp.where(blane < HALF, -1.0, 1.0)
    inv = 1.0 / train_count
    diag = blane == brow
    train = side_refs[0].shape[0]
    squares = jnp.zeros((1, LANES), jnp.float32)
    for side in side_refs:
        value = side[...].astype(jnp.float32)
        sums = jnp.sum(value * value, axis=0, keepdims=True)
        squares = squares + tree_sum([sums[:, j * LANES : (j + 1) * LANES] for j in range(blocks)])
    load = jnp.sum(squares, axis=1, keepdims=True) * (LOAD_EPS * inv / (blocks * HALF))

    def flip(i):
        for place, side in enumerate(side_refs):
            flipped[i * LANES : (i + 1) * LANES, place * train : (place + 1) * train] = side[
                :, i * LANES : (i + 1) * LANES
            ].T

    def gram(rows, cols):
        terms = [
            jnp.dot(
                flipped[rows, place * train : (place + 1) * train],
                side[:, cols],
                preferred_element_type=jnp.float32,
            )
            for place, side in enumerate(side_refs)
        ]
        return tree_sum(terms)

    def covariance(tile, on_diagonal):
        value = (pltpu.roll(tile[HALF:], HALF, 1) - tile[:HALF] * bsign) * inv
        return value + jnp.where(diag, load, 0.0) if on_diagonal else value

    def fill(j, count):
        tall = gram(slice(None), slice(j * LANES, (j + count) * LANES))
        for c in range(count):
            for i in range(blocks):
                tile = tall[i * LANES : (i + 1) * LANES, c * LANES : (c + 1) * LANES]
                mat[i * HALF : (i + 1) * HALF, (j + c) * LANES : (j + c + 1) * LANES] = covariance(
                    tile, i == j + c
                )

    mat[:, blocks * LANES :] = steer_ref[...]
    flip(0)
    norms = []
    pivot = covariance(gram(slice(0, LANES), slice(0, LANES)), True)
    jobs = [lambda i=i: flip(i) for i in range(1, blocks)]
    jobs += [lambda j=j: fill(j, min(2, blocks - j)) for j in range(0, blocks, 2)]
    jobs.append(lambda: prepare(0))

    def prepare(k):
        start = (k + 1) * LANES
        tile = mat[k * HALF : (k + 1) * HALF, start : start + LANES]
        turned = turn(tile, bsign)
        wide = jnp.concatenate(
            [jnp.concatenate([tile, turned], 1), jnp.concatenate([turned, -tile], 1)], 0
        )
        high, mid, low = three(wide)
        for place, part in enumerate((high, high, mid, mid, low, high)):
            next6[place * LANES : (place + 1) * LANES, :] = part
        if k + 1 < blocks:
            high, mid, low = three(mat[(k + 1) * HALF : (k + 2) * HALF, k * LANES : start])
            for place, part in enumerate((high, mid, high, low)):
                under[:, place * LANES : (place + 1) * LANES] = part

    def split_left(k, inverse):
        whole = jnp.concatenate([inverse, turn(inverse, bsign)], 0)
        scaled = exact_dot(mat[:, k * LANES : (k + 1) * LANES], whole)
        pieces = [scaled[: k * HALF], inverse, scaled[(k + 1) * HALF :]]
        scaled = jnp.concatenate(pieces if k else pieces[1:], 0)
        high, mid, low = three(scaled)
        for place, part in enumerate((high, mid, high, mid, high, low)):
            left6[:, place * LANES : (place + 1) * LANES] = part

    def split_right(k, tile):
        at = slice(tile * LANES, (tile + 1) * LANES)
        right = mat[k * HALF : (k + 1) * HALF, at]
        high, mid, low = three(jnp.concatenate([right, turn(right, bsign)], 0))
        for place, part in enumerate((high, high, mid, mid, low, high)):
            right6[place * LANES : (place + 1) * LANES, at] = part

    def update(k, tile, count):
        own = slice(k * HALF, (k + 1) * HALF)
        at = slice(tile * LANES, (tile + count) * LANES)
        change = jnp.dot(left6[...], right6[:, at], preferred_element_type=jnp.float32)
        if tile + count > blocks:
            norms.append(mat[own, blocks * LANES :] * change[own, -LANES:])
        if k:
            mat[: k * HALF, at] = mat[: k * HALF, at] - change[: k * HALF]
        mat[own, at] = change[own]
        below = slice((k + 1) * HALF, None)
        mat[below, at] = mat[below, at] - change[below]

    def packed_dot(pairs):
        out = None
        for a, b in pairs:
            term = jnp.dot(a, b, preferred_element_type=jnp.float32)
            out = term if out is None else out + term
        return out

    for k in range(blocks):
        tiles = [pivot[SUB * t : SUB * (t + 1)] for t in range(HALF // SUB)]
        panels = HALF // SUB

        def hook(t, jobs=jobs):
            for job in jobs[t * len(jobs) // panels : (t + 1) * len(jobs) // panels]:
                job()

        inverse = jnp.concatenate(invert_block(tiles, lane, sub, sign, hook), 0)
        start = (k + 1) * LANES
        high, mid, low = three(inverse)
        upper = jnp.concatenate([high, mid], 1)
        lower = jnp.concatenate([high, low], 1)
        first = packed_dot(
            [
                (upper, next6[0 : 2 * LANES, :]),
                (upper, next6[2 * LANES : 4 * LANES, :]),
                (lower, next6[4 * LANES :, :]),
            ]
        )
        if k + 1 < blocks:
            high, mid, low = three(jnp.concatenate([first[:, :LANES], first[:, LANES:]], 0))
            wide = jnp.concatenate([high, mid], 1)
            change = jnp.dot(
                under[:, : 2 * LANES], jnp.concatenate([wide, wide], 0), preferred_element_type=jnp.float32
            )
            change = change[:, :LANES] + change[:, LANES:]
            change = change + jnp.dot(
                under[:, 2 * LANES :], jnp.concatenate([low, high], 0), preferred_element_type=jnp.float32
            )
            pivot = mat[(k + 1) * HALF : (k + 2) * HALF, start : start + LANES] - change
            jobs = [lambda k=k, inverse=inverse: split_left(k, inverse)]
            for j in range(k + 1, blocks + 1, 2):
                count = min(2, blocks + 1 - j)
                for c in range(count):
                    jobs.append(lambda k=k, j=j, c=c: split_right(k, j + c))
                jobs.append(lambda k=k, j=j, count=count: update(k, j, count))
            jobs.append(lambda k=k: prepare(k + 1))
        else:
            own = slice(k * HALF, (k + 1) * HALF)
            norms.append(mat[own, start:] * first[:, :LANES])
            mat[own, start:] = first[:, :LANES]
            both = jnp.concatenate([first[:, :LANES], first[:, LANES:]], 0)
            above = slice(0, k * HALF)
            mat[above, start:] = mat[above, start:] - exact_dot(mat[above, k * LANES : start], both)
    norm = tree_sum(norms)
    total = jnp.sum(norm, axis=0, keepdims=True)
    total = total + pltpu.roll(jnp.broadcast_to(total, (SUB, LANES)), HALF, 1)[:1]
    low8 = (blane[:1] % HALF) < beams
    factor = jnp.where(low8, lax.rsqrt(jnp.where(low8, total, 1.0)), 0.0)
    weights = (mat[:, blocks * LANES :] * factor).astype(jnp.bfloat16)
    contract = (((0,), (1,)), ((), ()))
    real = lax.dot_general(weights, spec_ref[0], contract, preferred_element_type=jnp.float32)
    imag = lax.dot_general(weights, spec_ref[1], contract, preferred_element_type=jnp.float32)
    out_ref[0] = real[:beams] + imag[HALF : HALF + beams]
    out_ref[1] = real[HALF : HALF + beams] - imag[:beams]


def solve_and_filter(sides, steer, spectrum, train_count, beams):
    channels = sides[0].shape[1] // 2
    gates = spectrum.shape[1]
    width = 2 * channels + LANES
    return pl.pallas_call(
        lambda *refs: solve_kernel(train_count, beams, *refs),
        out_shape=jax.ShapeDtypeStruct((2, beams, gates), jnp.float32),
        in_specs=[pl.BlockSpec(memory_space=pltpu.VMEM)] * (2 + len(sides)),
        out_specs=pl.BlockSpec(memory_space=pltpu.VMEM),
        scratch_shapes=[
            pltpu.VMEM((channels, width), jnp.float32),
            pltpu.VMEM((channels, 6 * LANES), jnp.bfloat16),
            pltpu.VMEM((6 * LANES, width), jnp.bfloat16),
            pltpu.VMEM((6 * LANES, 2 * LANES), jnp.bfloat16),
            pltpu.VMEM((HALF, 4 * LANES), jnp.bfloat16),
            pltpu.VMEM((2 * channels, sum(side.shape[0] for side in sides)), jnp.bfloat16),
        ],
        compiler_params=pltpu.CompilerParams(vmem_limit_bytes=24 << 20),
        name="solve_and_filter",
    )(steer, spectrum, *sides)


def packed_steering(look_row, channels, angle_count):
    beams = look_row.shape[0]
    slope = 2 * look_row + 1 - angle_count
    half = jnp.pad(slope, (0, HALF - beams))
    lane = jnp.arange(LANES, dtype=jnp.int32)
    channel = jnp.arange(channels, dtype=jnp.int32)
    index = channel[:, None] * jnp.concatenate([half, half])[None, :]
    index = (index - jnp.where(lane >= HALF, angle_count // 2, 0)[None, :]) % (2 * angle_count)
    value = jnp.cos(index.astype(jnp.float32) * (math.pi / angle_count))
    return jnp.where((lane % HALF < beams)[None, :], value, 0.0)


def shift_pairs(count, stride, extent, hop):
    pairs = []
    for i in range(count):
        digit = i // stride % extent
        pairs.append((i, i + ((digit + hop) % extent - digit) * stride))
    return pairs


def gather_rows(rows, count):
    if count % 4:
        return (lax.all_gather(rows, "rng", axis=0, tiled=True),)
    outer = count // 4
    swap = shift_pairs(count, 2, 2, 1)
    pair = shift_pairs(count, 1, 2, 1)
    across = [lax.ppermute(rows, "rng", swap)]
    pieces = [rows]
    for hop in sorted(range(1, outer), key=lambda h: min(h, outer - h)):
        pieces.append(lax.ppermute(rows, "rng", shift_pairs(count, 4, outer, hop)))
    across += [lax.ppermute(piece, "rng", swap) for piece in pieces[1:]]
    side = jnp.concatenate(pieces + across, 0)
    return side, lax.ppermute(side, "rng", pair)


def on_device(radar_cube, train_gates, look_angles):
    dop = lax.axis_size("dop")
    rng = lax.axis_size("rng")
    local = radar_cube.shape[1]
    pulses = local * dop
    channels = radar_cube.shape[3]
    beams = look_angles.shape[1]
    classes = dop if local % dop == 0 else local
    parts = partial_spectra(radar_cube, doppler_table(dop, pulses), classes, dop)
    mine = [parts[0]]
    for hop in range(1, dop):
        pairs = [(d, (d + hop) % dop) for d in range(dop)]
        mine.append(lax.ppermute(parts[hop], "dop", pairs))
    spectrum, packed = finish_spectra(train_gates, mine, 1.0 / math.sqrt(pulses))
    sides = gather_rows(packed, rng)
    steer = packed_steering(look_angles[0], channels, NANG)
    out = solve_and_filter(sides, steer, spectrum, train_gates.shape[1] * rng, beams)
    return out[:, None]


def solution(mesh):
    placed = (P(None, "dop", "rng", None), P("dop", "rng"), P("dop", None))
    return jax.shard_map(
        on_device,
        mesh=mesh,
        in_specs=placed,
        out_specs=P(None, "dop", None, "rng"),
        check_vma=False,
    )
```

```python
import math

import jax
import jax.numpy as jnp
import numpy as np
from jax import lax
from jax.experimental import pallas as pl
from jax.experimental.pallas import tpu as pltpu
from jax.sharding import PartitionSpec as P

NANG = 256
LOAD_EPS = 1e-05
HALF = 64
LANES = 128
SUB = 8
HIGH = lax.Precision.HIGHEST


def doppler_table(bin_count, pulses):
    phase = (np.arange(bin_count)[:, None] * (pulses // bin_count) * np.arange(pulses)[None, :] % pulses) * (
        2.0 * math.pi / pulses
    )
    cosine = np.cos(phase).astype(np.float32).astype(jnp.bfloat16).astype(np.float32)
    sine = np.sin(phase).astype(np.float32).astype(jnp.bfloat16).astype(np.float32)
    upper = np.stack([cosine, sine], 1)
    lower = np.stack([-sine, cosine], 1)
    return np.stack([upper, lower], 0)


def pick(values, index):
    if all(v == values[0] for v in values):
        return float(values[0])
    out = jnp.float32(values[0])
    for i, v in enumerate(values[1:], 1):
        out = jnp.where(index == i, jnp.float32(v), out)
    return out


def partial_kernel(classes, dop, table, origin, *refs):
    cube_ref, *out_refs, buf, sems = refs
    me = lax.axis_index("dop")
    steps, _, local, step, width = buf.shape

    def copy(n):
        rows = pl.ds(pl.multiple_of(origin + n * step, step), step)
        return pltpu.make_async_copy(cube_ref.at[:, :, rows, :], buf.at[n], sems.at[n])

    for n in range(steps):
        copy(n).start()

    def body(n, carry):
        copy(n).wait()
        rows = pl.ds(pl.multiple_of(n * step, step), step)
        for base in range(0, width, LANES):
            cols = slice(base, base + LANES)
            folded = []
            for part in range(2):
                for cls in range(classes):
                    total = buf[n, part, cls, :, cols].astype(jnp.float32)
                    for pulse in range(cls + classes, local, classes):
                        total = total + buf[n, part, pulse, :, cols].astype(jnp.float32)
                    folded.append(total)
            for slot, out_ref in enumerate(out_refs):
                for row in range(2):
                    acc = None
                    for part in range(2):
                        for cls in range(classes):
                            options = [
                                table[row, (d + slot) % dop, part, d * local + cls] for d in range(dop)
                            ]
                            term = folded[part * classes + cls] * pick(options, me)
                            acc = term if acc is None else acc + term
                    out_ref[row, rows, cols] = acc.astype(out_ref.dtype)
        return carry

    lax.fori_loop(0, steps, body, 0)


def partial_spectra(cube, table, classes, dop, origin, gates):
    _, local, _, channels = cube.shape
    step = 16
    steps = gates // step
    return pl.pallas_call(
        lambda *refs: partial_kernel(classes, dop, table, origin, *refs),
        in_specs=[pl.BlockSpec(memory_space=pltpu.HBM)],
        out_specs=[pl.BlockSpec(memory_space=pltpu.VMEM)] * dop,
        out_shape=[
            jax.ShapeDtypeStruct((2, gates, channels), jnp.float32)
            for _ in range(dop)
        ],
        scratch_shapes=[
            pltpu.VMEM((steps, 2, local, step, channels), cube.dtype),
            pltpu.SemaphoreType.DMA((steps,)),
        ],
        compiler_params=pltpu.CompilerParams(vmem_limit_bytes=52 << 20),
        cost_estimate=pl.CostEstimate(
            flops=4 * local * gates * channels,
            transcendentals=0,
            bytes_accessed=4 * local * gates * channels,
        ),
        name="partial_spectra",
    )(cube)


def finish_kernel(scale, chunks, *refs):
    gates_ref, *parts, spec_ref, pack_ref = refs
    train = gates_ref.shape[1]
    gates = spec_ref.shape[1]
    shift = gates - train
    index = lax.broadcasted_iota(jnp.int32, (1, train), 1)
    same = jnp.where(gates_ref[...] == index, 1.0, 0.0)
    start = jnp.sum(same, axis=1, keepdims=True)
    row = lax.broadcasted_iota(jnp.int32, (train, LANES), 0).astype(jnp.float32)
    early = row < start
    lane = lax.broadcasted_iota(jnp.int32, (train, LANES), 1)
    low = lane < HALF
    for tile in range(spec_ref.shape[2] // LANES):
        cols = slice(tile * LANES, (tile + 1) * LANES)
        picked = []
        for part in range(2):
            stretches = []
            for chunk in range(chunks):
                group = parts[chunk * len(parts) // chunks : (chunk + 1) * len(parts) // chunks]
                stretches.append(tree_sum([ref[part, :, cols] for ref in group]))
            total = stretches[0] if chunks == 1 else jnp.concatenate(stretches, 0)
            value = (total * scale).astype(jnp.bfloat16)
            spec_ref[part, :, cols] = value
            value = value.astype(jnp.float32)
            picked.append(jnp.where(early, value[:train], value[shift:]))
        real, imag = picked
        first = jnp.where(low, real, pltpu.roll(imag, HALF, 1))
        second = jnp.where(low, pltpu.roll(real, HALF, 1), imag)
        base = 2 * tile * LANES
        pack_ref[:, base : base + LANES] = first.astype(jnp.bfloat16)
        pack_ref[:, base + LANES : base + 2 * LANES] = second.astype(jnp.bfloat16)


def finish_spectra(gate_row, parts, chunks, scale):
    _, gates, channels = parts[0].shape
    gates *= chunks
    train = gate_row.shape[1]
    return pl.pallas_call(
        lambda *refs: finish_kernel(scale, chunks, *refs),
        out_shape=(
            jax.ShapeDtypeStruct((2, gates, channels), jnp.bfloat16),
            jax.ShapeDtypeStruct((train, 2 * channels), jnp.bfloat16),
        ),
        in_specs=[pl.BlockSpec(memory_space=pltpu.VMEM)] * (1 + len(parts)),
        out_specs=[pl.BlockSpec(memory_space=pltpu.VMEM)] * 2,
        compiler_params=pltpu.CompilerParams(vmem_limit_bytes=8 << 20),
        name="finish_spectra",
    )(gate_row, *parts)


def spread(value, row):
    return jnp.broadcast_to(value[row : row + 1, :], (SUB, LANES))


def lane_spread(value, index, lane):
    kept = jnp.where(lane == index, value, 0.0)
    return jnp.broadcast_to(jnp.sum(kept, axis=1, keepdims=True), (SUB, LANES))


def tree_sum(terms):
    terms = list(terms)
    while len(terms) > 1:
        nxt = [terms[i] + terms[i + 1] for i in range(0, len(terms) - 1, 2)]
        if len(terms) % 2:
            nxt.append(terms[-1])
        terms = nxt
    return terms[0]


def invert_rows(real_cols, imag_cols, rows, turned, sub):
    recip = 1.0 / spread(real_cols[0], 0)
    scale = recip
    for j in range(SUB):
        own = sub == j
        if j:
            scale = jnp.where(own, recip, scale)
        cr = jnp.where(own, 0.0, real_cols[j])
        ci = jnp.where(own, 0.0, imag_cols[j])
        following = None
        if j + 1 < SUB:
            ur = spread(real_cols[j + 1], j)
            ui = spread(imag_cols[j + 1], j)
            real_cols[j + 1] = real_cols[j + 1] - (cr * ur - ci * ui) * recip
            imag_cols[j + 1] = imag_cols[j + 1] - (cr * ui + ci * ur) * recip
            following = 1.0 / spread(real_cols[j + 1], j + 1)
        sr = cr * recip
        si = ci * recip
        for l in range(j + 2, SUB):
            ur = spread(real_cols[l], j)
            ui = spread(imag_cols[l], j)
            real_cols[l] = real_cols[l] - (sr * ur - si * ui)
            imag_cols[l] = imag_cols[l] - (sr * ui + si * ur)
        one = spread(rows, j)
        two = spread(turned, j)
        rows = rows - (sr * one + si * two)
        turned = turned - (sr * two - si * one)
        recip = following
    return rows * scale, turned * scale


def invert_block(tiles, lane, sub, sign, hook):
    count = len(tiles)
    for t in range(count):
        k = SUB * t
        in_re = (lane >= k) & (lane < k + SUB)
        in_im = (lane >= HALF + k) & (lane < HALF + k + SUB)
        inside = in_re | in_im
        real_cols, imag_cols = [], []
        for l in range(SUB):
            real_cols.append(lane_spread(tiles[t], k + l, lane))
            imag_cols.append(lane_spread(tiles[t], HALF + k + l, lane))
        unit = jnp.where(in_re & (lane - k == sub), 1.0, 0.0)
        rows = jnp.where(inside, unit, tiles[t])
        turned = pltpu.roll(rows, HALF, 1) * sign
        rows, turned = invert_rows(real_cols, imag_cols, rows, turned, sub)
        ones = [spread(rows, l) for l in range(SUB)]
        twos = [spread(turned, l) for l in range(SUB)]
        fresh = list(tiles)
        fresh[t] = rows
        for i in list(range(t + 1, count)) + list(range(t)):
            terms = []
            for l in range(SUB):
                cr = lane_spread(tiles[i], k + l, lane)
                ci = lane_spread(tiles[i], HALF + k + l, lane)
                terms.append(cr * ones[l] + ci * twos[l])
            fresh[i] = jnp.where(inside, 0.0, tiles[i]) - tree_sum(terms)
        tiles = fresh
        hook(t)
    return tiles


def turn(value, sign):
    tiles = value.shape[1] // LANES
    out = [
        pltpu.roll(value[:, t * LANES : (t + 1) * LANES], HALF, 1) * sign[: value.shape[0]]
        for t in range(tiles)
    ]
    return out[0] if tiles == 1 else jnp.concatenate(out, 1)


def exact_dot(a, b):
    return jnp.dot(a, b, precision=HIGH, preferred_element_type=jnp.float32)


def three(value):
    high = value.astype(jnp.bfloat16)
    rest = value - high.astype(jnp.float32)
    mid = rest.astype(jnp.bfloat16)
    return high, mid, (rest - mid.astype(jnp.float32)).astype(jnp.bfloat16)


def solve_kernel(train_count, beams, steer_ref, spec_ref, *refs):
    *side_refs, out_ref, mat, left6, right6, next6, under, flipped = refs
    blocks = mat.shape[0] // HALF
    lane = lax.broadcasted_iota(jnp.int32, (SUB, LANES), 1)
    sub = lax.broadcasted_iota(jnp.int32, (SUB, LANES), 0)
    sign = jnp.where(lane < HALF, -1.0, 1.0)
    blane = lax.broadcasted_iota(jnp.int32, (HALF, LANES), 1)
    brow = lax.broadcasted_iota(jnp.int32, (HALF, LANES), 0)
    bsign = jnp.where(blane < HALF, -1.0, 1.0)
    inv = 1.0 / train_count
    diag = blane == brow
    train = side_refs[0].shape[0]
    squares = jnp.zeros((1, LANES), jnp.float32)
    for side in side_refs:
        value = side[...].astype(jnp.float32)
        sums = jnp.sum(value * value, axis=0, keepdims=True)
        squares = squares + tree_sum([sums[:, j * LANES : (j + 1) * LANES] for j in range(blocks)])
    load = jnp.sum(squares, axis=1, keepdims=True) * (LOAD_EPS * inv / (blocks * HALF))

    def flip(i):
        for place, side in enumerate(side_refs):
            flipped[i * LANES : (i + 1) * LANES, place * train : (place + 1) * train] = side[
                :, i * LANES : (i + 1) * LANES
            ].T

    def gram(rows, cols):
        terms = [
            jnp.dot(
                flipped[rows, place * train : (place + 1) * train],
                side[:, cols],
                preferred_element_type=jnp.float32,
            )
            for place, side in enumerate(side_refs)
        ]
        return tree_sum(terms)

    def covariance(tile, on_diagonal):
        value = (pltpu.roll(tile[HALF:], HALF, 1) - tile[:HALF] * bsign) * inv
        return value + jnp.where(diag, load, 0.0) if on_diagonal else value

    def fill(j, count):
        tall = gram(slice(None), slice(j * LANES, (j + count) * LANES))
        for c in range(count):
            for i in range(blocks):
                tile = tall[i * LANES : (i + 1) * LANES, c * LANES : (c + 1) * LANES]
                mat[i * HALF : (i + 1) * HALF, (j + c) * LANES : (j + c + 1) * LANES] = covariance(
                    tile, i == j + c
                )

    mat[:, blocks * LANES :] = steer_ref[...]
    flip(0)
    norms = []
    pivot = covariance(gram(slice(0, LANES), slice(0, LANES)), True)
    ahead = {}
    jobs = [lambda i=i: flip(i) for i in range(1, blocks)]
    jobs += [lambda j=j: fill(j, min(2, blocks - j)) for j in range(0, blocks, 2)]
    jobs.append(lambda: prepare(0))

    def prepare(k):
        start = (k + 1) * LANES
        tile = mat[k * HALF : (k + 1) * HALF, start : start + LANES]
        turned = turn(tile, bsign)
        wide = jnp.concatenate(
            [jnp.concatenate([tile, turned], 1), jnp.concatenate([turned, -tile], 1)], 0
        )
        high, mid, low = three(wide)
        for place, part in enumerate((high, high, mid, mid, low, high)):
            next6[place * LANES : (place + 1) * LANES, :] = part
        if k + 1 < blocks:
            high, mid, low = three(mat[(k + 1) * HALF : (k + 2) * HALF, k * LANES : start])
            for place, part in enumerate((high, mid, high, low)):
                under[:, place * LANES : (place + 1) * LANES] = part

    def split_left(k, inverse):
        whole = jnp.concatenate([inverse, turn(inverse, bsign)], 0)
        scaled = exact_dot(mat[:, k * LANES : (k + 1) * LANES], whole)
        pieces = [scaled[: k * HALF], inverse, scaled[(k + 1) * HALF :]]
        scaled = jnp.concatenate(pieces if k else pieces[1:], 0)
        high, mid, low = three(scaled)
        for place, part in enumerate((high, mid, high, mid, high, low)):
            left6[:, place * LANES : (place + 1) * LANES] = part

    def split_right(k, tile):
        at = slice(tile * LANES, (tile + 1) * LANES)
        right = mat[k * HALF : (k + 1) * HALF, at]
        high, mid, low = three(jnp.concatenate([right, turn(right, bsign)], 0))
        for place, part in enumerate((high, high, mid, mid, low, high)):
            right6[place * LANES : (place + 1) * LANES, at] = part

    def update(k, tile, count):
        own = slice(k * HALF, (k + 1) * HALF)
        at = slice(tile * LANES, (tile + count) * LANES)
        change = jnp.dot(left6[...], right6[:, at], preferred_element_type=jnp.float32)
        if tile + count > blocks:
            norms.append(mat[own, blocks * LANES :] * change[own, -LANES:])
        if k:
            mat[: k * HALF, at] = mat[: k * HALF, at] - change[: k * HALF]
        mat[own, at] = change[own]
        below = slice((k + 1) * HALF, None)
        mat[below, at] = mat[below, at] - change[below]

    def packed_dot(pairs):
        out = None
        for a, b in pairs:
            term = jnp.dot(a, b, preferred_element_type=jnp.float32)
            out = term if out is None else out + term
        return out

    for k in range(blocks):
        tiles = [pivot[SUB * t : SUB * (t + 1)] for t in range(HALF // SUB)]
        panels = HALF // SUB

        def hook(t, jobs=jobs):
            for job in jobs[t * len(jobs) // panels : (t + 1) * len(jobs) // panels]:
                job()

        inverse = jnp.concatenate(invert_block(tiles, lane, sub, sign, hook), 0)
        start = (k + 1) * LANES
        high, mid, low = three(inverse)
        upper = jnp.concatenate([high, mid], 1)
        lower = jnp.concatenate([high, low], 1)
        first = packed_dot(
            [
                (upper, next6[0 : 2 * LANES, :]),
                (upper, next6[2 * LANES : 4 * LANES, :]),
                (lower, next6[4 * LANES :, :]),
            ]
        )
        if k + 1 < blocks:
            high, mid, low = three(jnp.concatenate([first[:, :LANES], first[:, LANES:]], 0))
            wide = jnp.concatenate([high, mid], 1)
            change = jnp.dot(
                under[:, : 2 * LANES], jnp.concatenate([wide, wide], 0), preferred_element_type=jnp.float32
            )
            change = change[:, :LANES] + change[:, LANES:]
            change = change + jnp.dot(
                under[:, 2 * LANES :], jnp.concatenate([low, high], 0), preferred_element_type=jnp.float32
            )
            pivot = mat[(k + 1) * HALF : (k + 2) * HALF, start : start + LANES] - change
            jobs = [lambda k=k, inverse=inverse: split_left(k, inverse)]
            for j in range(k + 1, blocks + 1, 2):
                count = min(2, blocks + 1 - j)
                for c in range(count):
                    jobs.append(lambda k=k, j=j, c=c: split_right(k, j + c))
                jobs.append(lambda k=k, j=j, count=count: update(k, j, count))
            jobs.append(lambda k=k: prepare(k + 1))
        else:
            own = slice(k * HALF, (k + 1) * HALF)
            norms.append(mat[own, start:] * first[:, :LANES])
            mat[own, start:] = first[:, :LANES]
            both = jnp.concatenate([first[:, :LANES], first[:, LANES:]], 0)
            above = slice(0, k * HALF)
            mat[above, start:] = mat[above, start:] - exact_dot(mat[above, k * LANES : start], both)
    norm = tree_sum(norms)
    total = jnp.sum(norm, axis=0, keepdims=True)
    total = total + pltpu.roll(jnp.broadcast_to(total, (SUB, LANES)), HALF, 1)[:1]
    low8 = (blane[:1] % HALF) < beams
    factor = jnp.where(low8, lax.rsqrt(jnp.where(low8, total, 1.0)), 0.0)
    weights = (mat[:, blocks * LANES :] * factor).astype(jnp.bfloat16)
    contract = (((0,), (1,)), ((), ()))
    real = lax.dot_general(weights, spec_ref[0], contract, preferred_element_type=jnp.float32)
    imag = lax.dot_general(weights, spec_ref[1], contract, preferred_element_type=jnp.float32)
    out_ref[0] = real[:beams] + imag[HALF : HALF + beams]
    out_ref[1] = real[HALF : HALF + beams] - imag[:beams]


def solve_and_filter(sides, steer, spectrum, train_count, beams):
    channels = sides[0].shape[1] // 2
    gates = spectrum.shape[1]
    width = 2 * channels + LANES
    return pl.pallas_call(
        lambda *refs: solve_kernel(train_count, beams, *refs),
        out_shape=jax.ShapeDtypeStruct((2, beams, gates), jnp.float32),
        in_specs=[pl.BlockSpec(memory_space=pltpu.VMEM)] * (2 + len(sides)),
        out_specs=pl.BlockSpec(memory_space=pltpu.VMEM),
        scratch_shapes=[
            pltpu.VMEM((channels, width), jnp.float32),
            pltpu.VMEM((channels, 6 * LANES), jnp.bfloat16),
            pltpu.VMEM((6 * LANES, width), jnp.bfloat16),
            pltpu.VMEM((6 * LANES, 2 * LANES), jnp.bfloat16),
            pltpu.VMEM((HALF, 4 * LANES), jnp.bfloat16),
            pltpu.VMEM((2 * channels, sum(side.shape[0] for side in sides)), jnp.bfloat16),
        ],
        compiler_params=pltpu.CompilerParams(vmem_limit_bytes=24 << 20),
        name="solve_and_filter",
    )(steer, spectrum, *sides)


def packed_steering(look_row, channels, angle_count):
    beams = look_row.shape[0]
    slope = 2 * look_row + 1 - angle_count
    half = jnp.pad(slope, (0, HALF - beams))
    lane = jnp.arange(LANES, dtype=jnp.int32)
    channel = jnp.arange(channels, dtype=jnp.int32)
    index = channel[:, None] * jnp.concatenate([half, half])[None, :]
    index = (index - jnp.where(lane >= HALF, angle_count // 2, 0)[None, :]) % (2 * angle_count)
    value = jnp.cos(index.astype(jnp.float32) * (math.pi / angle_count))
    return jnp.where((lane % HALF < beams)[None, :], value, 0.0)


def shift_pairs(count, stride, extent, hop):
    pairs = []
    for i in range(count):
        digit = i // stride % extent
        pairs.append((i, i + ((digit + hop) % extent - digit) * stride))
    return pairs


def gather_rows(rows, count):
    if count % 4:
        return (lax.all_gather(rows, "rng", axis=0, tiled=True),)
    outer = count // 4
    swap = shift_pairs(count, 2, 2, 1)
    pair = shift_pairs(count, 1, 2, 1)
    across = [lax.ppermute(rows, "rng", swap)]
    pieces = [rows]
    for hop in sorted(range(1, outer), key=lambda h: min(h, outer - h)):
        pieces.append(lax.ppermute(rows, "rng", shift_pairs(count, 4, outer, hop)))
    across += [lax.ppermute(piece, "rng", swap) for piece in pieces[1:]]
    side = jnp.concatenate(pieces + across, 0)
    return side, lax.ppermute(side, "rng", pair)


def on_device(radar_cube, train_gates, look_angles):
    dop = lax.axis_size("dop")
    rng = lax.axis_size("rng")
    local = radar_cube.shape[1]
    pulses = local * dop
    channels = radar_cube.shape[3]
    beams = look_angles.shape[1]
    classes = dop if local % dop == 0 else local
    table = doppler_table(dop, pulses)
    gates = radar_cube.shape[2]
    chunks = 2 if gates % 32 == 0 else 1
    chunk = gates // chunks
    mine = []
    for c in range(chunks):
        parts = partial_spectra(radar_cube, table, classes, dop, c * chunk, chunk)
        mine.append(parts[0])
        for hop in range(1, dop):
            pairs = [(d, (d + hop) % dop) for d in range(dop)]
            mine.append(lax.ppermute(parts[hop], "dop", pairs))
    spectrum, packed = finish_spectra(train_gates, mine, chunks, 1.0 / math.sqrt(pulses))
    sides = gather_rows(packed, rng)
    steer = packed_steering(look_angles[0], channels, NANG)
    out = solve_and_filter(sides, steer, spectrum, train_gates.shape[1] * rng, beams)
    return out[:, None]


def solution(mesh):
    placed = (P(None, "dop", "rng", None), P("dop", "rng"), P("dop", None))
    return jax.shard_map(
        on_device,
        mesh=mesh,
        in_specs=placed,
        out_specs=P(None, "dop", None, "rng"),
        check_vma=False,
    )
```
